512 devices in a mesh: slab: 16 (over z, core), col: 32 (over y, x).
Axes of the slice: x: 4, y: 8, z: 8, core: 2. Of those that a mesh axis runs over, the one named last changes fastest.
Arguments:
- field: bfloat16 [2, 256, 1024, 1024], P(None, 'slab', 'col'), may hold values from -6 to 6
- fine_plane: int32 [128, 1024, 1024], P('slab', 'col'), may hold values from 0 to 15, as said below
- fine_frac: int32 [128, 1024, 1024], P('slab', 'col'), may hold values from 0 to 7
- counts: int32 [16, 1024, 1024], P('slab', 'col'), may hold values from 1 to 8
Outputs:
- fine_color: float32 [1024, 1024], P('col', 'slab')
- fine_depth: float32 [1024, 1024], P('col', 'slab')
- coarse_color: float32 [1024, 1024], P('col', 'slab')
The draws below stay inside these ranges and needn't reach their ends.
Inputs may be any that keep to these rules, and one draw needn't show every extreme that they name: For each ray and slab the positions 8 * fine_plane + fine_frac are nondecreasing over the 8 slots.
All inputs are finite; a program needn't handle non-finite values.
Results may differ from the reference program's by a relative error of at most 0.0003.
Values may be sent and summed in bfloat16 or wider, within the bound.
A program may use at most 64 MiB of HBM per device.

```python
import jax
import jax.numpy as jnp
from jax import lax

DEPTH_DEV = 16
U_DEV = 32
V = 1024
FINE = 8
NZ = 256
NU = 1024
N_SLAB = 16
N_COL = 32


def fine_positions(key):
    slabs = NZ // DEPTH_DEV
    inner = jax.random.fold_in(key, 1013)
    spots = jax.random.randint(inner, (slabs, FINE, NU, V), 0, DEPTH_DEV * 8, dtype=jnp.int32)
    spots = jnp.sort(spots, axis=1)
    return spots.reshape(slabs * FINE, NU, V)


def draw_fine_plane(key, part):
    return fine_positions(key) // 8


def draw_fine_frac(key, part):
    return fine_positions(key) % 8


def set_ends(entries, stream_key, low, top_value):
    longest = entries.shape.index(max(entries.shape))
    spots = []
    for shift in (0, 1):
        where = [jax.random.randint(jax.random.fold_in(stream_key, axis), (), 0, length) for axis, length in enumerate(entries.shape)]
        where[longest] = (where[longest] + shift) % entries.shape[longest]
        spots.append(tuple(where))
    return entries.at[spots[0]].set(low).at[spots[1]].set(top_value)


def block_scale(rng, dims, cuts, least, largest):
    gain, own = 1.0, jax.random.fold_in(rng, 6)
    for axis_at, blocks in cuts:
        draws = jnp.exp(jax.random.uniform(jax.random.fold_in(own, axis_at), (blocks,), jnp.float32, least / len(cuts), largest / len(cuts)))
        gain = gain * jnp.repeat(draws, dims[axis_at] // blocks).reshape([-1 if axis == axis_at else 1 for axis in range(len(dims))])
    return gain


def bell_draw(stream_key, shape, width, reach, shards=(), kind=jnp.bfloat16):
    factor_of = block_scale(stream_key, shape, shards, -0.22, 0.18) if shards else 1.0
    entries = jax.random.normal(stream_key, shape, jnp.float32) * width * factor_of
    return jnp.minimum(jnp.maximum(entries, -reach), reach).astype(kind)


def setup_inputs(seed: int = 0) -> dict:
    key_list = jax.random.split(jax.random.key(seed), 5)
    return {
        "field": bell_draw(key_list[0], (2, NZ, NU, V), 1.0, 6.0, ((1, 16), (2, 32))),
        "fine_plane": draw_fine_plane(jax.random.fold_in(key_list[4], 71), 0),
        "fine_frac": draw_fine_frac(jax.random.fold_in(key_list[4], 71), 0),
        "counts": set_ends(jax.random.randint(key_list[3], (N_SLAB, NU, V), 1, FINE + 1), jax.random.fold_in(key_list[3], 1), 1, FINE).astype(jnp.int32),
    }


def shade(values):
    density = (2.0 / NZ) * jax.nn.softplus(values[0])
    emission = jax.nn.sigmoid(values[1])
    return density, emission


def exclusive_product(factor):
    totals = jnp.cumprod(factor, axis=0)
    return jnp.concatenate([jnp.ones_like(factor[:1]), totals[:-1]], axis=0)


def render_rows(field_rows, plane_rows, frac_rows, count_rows):
    empty = jnp.zeros((2, 1) + field_rows.shape[2:], jnp.bfloat16)
    volume = jnp.concatenate([field_rows, empty], axis=1)
    lower = volume[:, 7:NZ:8].astype(jnp.float32)
    upper = volume[:, 8:NZ + 1:8].astype(jnp.float32)
    density, emission = shade(0.5 * (lower + upper))
    factor = jnp.exp(-8.0 * density)
    opacity = 1.0 - factor
    coarse = jnp.sum(exclusive_product(factor) * opacity * emission, axis=0)
    slots = plane_rows.shape[0]
    slab_of = (jnp.arange(slots, dtype=jnp.int32) // FINE).astype(jnp.int32)
    start = plane_rows + (slab_of * DEPTH_DEV)[:, None, None]
    index = jnp.broadcast_to(start[None], (2,) + start.shape)
    low = jnp.take_along_axis(volume, index, axis=1).astype(jnp.float32)
    high = jnp.take_along_axis(volume, index + 1, axis=1).astype(jnp.float32)
    weight = frac_rows.astype(jnp.float32) / 8.0
    values = (1.0 - weight) * low + weight * high
    density, emission = shade(values)
    position = (jnp.arange(slots, dtype=jnp.int32) % FINE)[:, None, None]
    live = position < jnp.repeat(count_rows, FINE, axis=0)
    factor = jnp.where(live, jnp.exp(-(DEPTH_DEV / FINE) * density), jnp.float32(1.0))
    opacity = 1.0 - factor
    weighted = exclusive_product(factor) * opacity
    color = jnp.sum(weighted * emission, axis=0)
    depth = jnp.sum(weighted * ((start.astype(jnp.float32) + weight) / NZ), axis=0)
    return jnp.stack([color, depth, coarse])


def reference(field, fine_plane, fine_frac, counts):
    def one_block(block):
        first = (block * U_DEV).astype(jnp.int32)
        return render_rows(
            lax.dynamic_slice_in_dim(field, first, U_DEV, 2),
            lax.dynamic_slice_in_dim(fine_plane, first, U_DEV, 1),
            lax.dynamic_slice_in_dim(fine_frac, first, U_DEV, 1),
            lax.dynamic_slice_in_dim(counts, first, U_DEV, 1))

    blocks = lax.map(one_block, jnp.arange(N_COL, dtype=jnp.int32))
    images = jnp.concatenate([blocks[k] for k in range(N_COL)], axis=1)
    padded = jnp.pad(images, ((0, 0), (1, 1), (0, 0)))
    smooth = 0.25 * padded[:, :-2] + 0.5 * padded[:, 1:-1] + 0.25 * padded[:, 2:]
    return smooth[0], smooth[1], smooth[2]
```

```python
import jax
import jax.numpy as jnp
from jax import lax
from jax.experimental import pallas as pl
from jax.experimental.pallas import tpu as pltpu
from jax.sharding import PartitionSpec as P

F32 = jnp.float32
MESH = pl.DeviceIdType.MESH
LANES = 128
HALF = 16
LOG2E = 1.4426950408889634
SHIFT = 0.5
TOP = 65535.0
COLOR_SPAN = (-22.5, 0.0)
DEPTH_SPAN = (-15.0, 10.75)


def pick(leaves, masks):
    for mask in masks:
        pairs = [jnp.where(mask, leaves[i + 1], leaves[i]) for i in range(0, len(leaves) - 1, 2)]
        leaves = pairs + leaves[2 * len(pairs) :]
    return leaves[0]


def softplus2(values):
    return jnp.log2(1.0 + jnp.exp2(values * LOG2E))


def march_group(field, halo, planes, fracs, counts, rows, cols, slab):
    depth = field.shape[1]
    slots = planes.shape[0]
    total = depth * 16
    scale = 2.0 / total

    def leaf(channel, plane):
        if plane == depth:
            return halo[channel, rows, cols]
        return field[channel, plane, rows, cols]

    shape = (HALF, LANES)
    live = counts[0, rows, cols]
    through, color, reach = jnp.ones(shape, F32), jnp.zeros(shape, F32), jnp.zeros(shape, F32)
    first = (slab * depth * 8).astype(F32) + SHIFT
    i16 = jnp.int16
    for slot in range(slots):
        plane = planes[slot, rows, cols]
        spot = (plane << 3) + fracs[slot, rows, cols]
        p = plane.astype(i16)
        up = p + i16(1)
        odd_bits = [(p & i16(2)) != i16(0), (p & i16(4)) != i16(0), p >= i16(8)]
        even_bits = [(up & i16(2)) != i16(0), (up & i16(4)) != i16(0), up >= i16(8), up >= i16(16)]
        even_weight = jnp.abs((spot & 15).astype(F32) * 0.125 - 1.0)
        values = []
        for channel in range(2):
            odd = pick([leaf(channel, k) for k in range(1, depth, 2)], odd_bits).astype(F32)
            even = pick([leaf(channel, k) for k in range(0, depth + 1, 2)], even_bits).astype(F32)
            values.append(odd + (even - odd) * even_weight)
        factor = jnp.exp2(softplus2(values[0]) * (-scale * depth / slots))
        after = through * jnp.where(live > slot, factor, 1.0)
        weight = through - after
        through = after
        color = color + weight * (1.0 + jnp.tanh(0.5 * values[1]))
        reach = reach + weight * (spot.astype(F32) + first)
    coarse_through, coarse = jnp.ones(shape, F32), jnp.zeros(shape, F32)
    for k in range(7, depth, 8):
        value, shine = [
            0.5 * (leaf(channel, k).astype(F32) + leaf(channel, k + 1).astype(F32)) for channel in range(2)
        ]
        after = coarse_through * jnp.exp2(softplus2(value) * (-8.0 * scale))
        coarse = coarse + (coarse_through - after) * (1.0 + jnp.tanh(0.5 * shine))
        coarse_through = after
    return 0.5 * color, reach, through, 0.5 * coarse, coarse_through


def as_code(u):
    return (jnp.clip(u, 0.0, TOP) + 0.5).astype(jnp.int32)


def encode_log(values, span):
    low, high = span
    step = TOP / (high - low)
    return as_code(jnp.log2(values) * step - low * step)


def decode_log(code, span):
    low, high = span
    return jnp.exp2(code.astype(F32) * ((high - low) / TOP) + low)


def kernel(
    field_in, plane_in, frac_in, count_in,
    image_out,
    field, halo, planes, fracs, counts, mine, sent, partner, packed, got, image,
    load_sem, halo_send, halo_recv, pair_send, pair_recv, chip_send, chip_recv, edge_send, edge_recv, behind, told,
):
    slab, col = lax.axis_index("slab"), lax.axis_index("col")
    slabs, columns = lax.axis_size("slab"), lax.axis_size("col")
    chips = slabs // 2
    z, core = slab // 2, slab % 2
    other = slab + 1 - 2 * core
    tiles = chips

    def device(s, c):
        return {"slab": s, "col": c}

    def order(chip, i):
        away = chips // 2 + jnp.where(i % 2 == 1, -1, 1) * ((i + 1) // 2)
        return lax.rem(chip + away, chips)

    def lanes(tile):
        return pl.ds(pl.multiple_of(tile * LANES, LANES), LANES)

    def loads(i):
        cols = lanes(order(z, i))
        return [
            pltpu.make_async_copy(field_in.at[:, :, :, cols], field.at[:, :, :, cols], load_sem.at[0, i]),
            pltpu.make_async_copy(plane_in.at[:, :, cols], planes.at[:, :, cols], load_sem.at[1, i]),
            pltpu.make_async_copy(frac_in.at[:, :, cols], fracs.at[:, :, cols], load_sem.at[2, i]),
            pltpu.make_async_copy(count_in.at[:, :, cols], counts.at[:, :, cols], load_sem.at[3, i]),
        ]

    barrier = pltpu.get_barrier_semaphore()

    def tell(semaphore, s, c):
        pl.semaphore_signal(semaphore, inc=1, device_id=device(s, c), device_id_type=MESH)

    tell(barrier, other, col)
    for away in range(1, chips):

        @pl.when(z < chips - away)
        def _():
            tell(barrier, slab + 2 * away, col)

    @pl.when(jnp.logical_and(core == 1, z < chips - 1))
    def _():
        tell(barrier, slab + 1, col)

    @pl.when(col > 0)
    def _():
        tell(barrier, 2 * z + 1, col - 1)

    @pl.when(col < columns - 1)
    def _():
        tell(barrier, 2 * z + 1, col + 1)

    for copy in loads(0):
        copy.start()

    def count(*conditions):
        return sum(jnp.where(c, 1, 0) for c in conditions)

    from_columns = 2 * core * count(col > 0, col < columns - 1)
    pl.semaphore_wait(barrier, 1 + z + (1 - core) * count(z > 0) + from_columns)

    def front_copy(to, i):
        cols = lanes(order(to // 2, i))
        return pltpu.make_async_remote_copy(
            src_ref=field_in.at[:, 0, :, cols], dst_ref=halo.at[:, :, cols],
            send_sem=halo_send.at[i], recv_sem=halo_recv.at[i],
            device_id=device(to, col), device_id_type=MESH,
        )

    @pl.when(slab > 0)
    def _():
        def start_front(i, _):
            front_copy(slab - 1, i).start()
            return 0

        lax.fori_loop(0, tiles, start_front, 0)

    for away in range(1, chips):

        @pl.when(z >= away)
        def _():
            tell(behind, slab - 2 * away, col)

    @pl.when(core == 1)
    def _():
        tell(told, other, col)

    def start_loads(i, _):
        for copy in loads(i):
            copy.start()
        return 0

    lax.fori_loop(1, tiles, start_loads, 0)

    @pl.when(slab == slabs - 1)
    def _():
        halo[...] = jnp.zeros_like(halo)

    patience = jnp.minimum(tiles, 3 * jnp.maximum(chips - 2 - z, 0))

    def hear_behind():
        pl.semaphore_wait(behind, chips - 1 - z)

    def pair_copy(i):
        return pltpu.make_async_remote_copy(
            src_ref=sent.at[i], dst_ref=partner.at[i],
            send_sem=pair_send.at[i], recv_sem=pair_recv.at[i],
            device_id=device(other, col), device_id_type=MESH,
        )

    def chip_copy(i):
        return pltpu.make_async_remote_copy(
            src_ref=packed.at[i], dst_ref=got.at[z],
            send_sem=chip_send.at[i], recv_sem=chip_recv.at[z],
            device_id=device(2 * order(z, i) + core, col), device_id_type=MESH,
        )

    def march(i, ref, half):
        rows = pl.ds(pl.multiple_of(half * HALF, HALF), HALF)
        parts = march_group(field, halo, planes, fracs, counts, rows, lanes(order(z, i)), slab)
        for n, part in enumerate(parts):
            ref[i, n] = part

    def join(i):
        pair_copy(i).wait_recv()
        words = []
        halves = []
        for rows in (pl.ds(0, 8), pl.ds(8, 8)):
            own = [mine[i, n, rows] for n in range(5)]
            far = [partner[i, n, rows] for n in range(5)]
            front = [jnp.where(core == 0, a, b) for a, b in zip(own, far)]
            back = [jnp.where(core == 0, b, a) for a, b in zip(own, far)]
            color = front[0] + front[2] * back[0]
            reach = front[1] + front[2] * back[1]
            coarse = front[3] + front[4] * back[3]
            halves.append([
                encode_log(color, COLOR_SPAN), encode_log(reach, DEPTH_SPAN), as_code(front[2] * back[2] * TOP),
                encode_log(coarse, COLOR_SPAN), as_code(front[4] * back[4] * TOP),
            ])
        for upper, lower in zip(*halves):
            words.append(upper | (lower << 16))
        return words

    def ready(i):
        for copy in loads(i):
            copy.wait()

        @pl.when(slab < slabs - 1)
        def _():
            front_copy(slab, i).wait_recv()

        march(i, sent, 1 - core)
        pair_copy(i).start()

    def step(i, _):
        ready(i + 1)
        march(i, mine, core)

        @pl.when(jnp.logical_and(i == patience, z < chips - 1))
        def _():
            hear_behind()

        for n, word in enumerate(join(i)):
            packed[i, n] = word

        @pl.when(jnp.logical_or(order(z, i) < z, i >= patience))
        def _():
            chip_copy(i).start()

        return 0

    ready(0)
    lax.fori_loop(0, tiles - 1, step, 0)
    march(tiles - 1, mine, core)

    @pl.when(patience >= tiles - 1)
    def _():
        hear_behind()

    def late(i, _):
        @pl.when(jnp.logical_and(order(z, i) > z, i < patience))
        def _():
            chip_copy(i).start()

        return 0

    lax.fori_loop(0, tiles - 1, late, 0)
    for n, word in enumerate(join(tiles - 1)):
        got[z, n] = word

    @pl.when(slab > 0)
    def _():
        def end_front(i, _):
            front_copy(slab - 1, i).wait_send()
            return 0

        lax.fori_loop(0, tiles, end_front, 0)

    def end_pair(i, _):
        pair_copy(i).wait_send()
        return 0

    lax.fori_loop(0, tiles, end_pair, 0)

    def end_chip(i, _):
        chip_copy(i).wait_send()
        return 0

    lax.fori_loop(0, tiles - 1, end_chip, 0)

    @pl.when(core == 0)
    def _():
        pl.semaphore_wait(told, 1)

    shape = (8, LANES)
    state = [[jnp.ones(shape, F32), jnp.ones(shape, F32)] + [jnp.zeros(shape, F32)] * 3 for _ in range(2)]
    for chip in range(chips):

        @pl.when(z != chip)
        def _():
            pltpu.make_async_remote_copy(
                src_ref=packed.at[0], dst_ref=got.at[chip], send_sem=chip_send.at[0], recv_sem=chip_recv.at[chip],
                device_id=device(slab, col), device_id_type=MESH,
            ).wait_recv()

        words = [got[chip, n] for n in range(5)]
        for half in range(2):
            codes = [(w & 0xFFFF) if half == 0 else (lax.shift_right_logical(w, 16)) for w in words]
            fine, plain, color, reach, coarse = state[half]
            color = color + fine * decode_log(codes[0], COLOR_SPAN)
            reach = reach + fine * decode_log(codes[1], DEPTH_SPAN)
            coarse = coarse + plain * decode_log(codes[3], COLOR_SPAN)
            fine = fine * (codes[2].astype(F32) * (1.0 / TOP))
            plain = plain * (codes[4].astype(F32) * (1.0 / TOP))
            state[half] = [fine, plain, color, reach, coarse]
    for half in range(2):
        fine, plain, color, reach, coarse = state[half]
        rows = pl.ds(pl.multiple_of(8 + core * HALF + 8 * half, 8), 8)
        image[0, rows] = color
        image[1, rows] = (reach - SHIFT * (1.0 - fine)) * (1.0 / 2048)
        image[2, rows] = coarse

    def rows_copy(n, first, target_first, count, s, c):
        return pltpu.make_async_remote_copy(
            src_ref=image.at[:, pl.ds(pl.multiple_of(first, 8), count)],
            dst_ref=image.at[:, pl.ds(pl.multiple_of(target_first, 8), count)],
            send_sem=edge_send.at[n], recv_sem=edge_recv.at[n if n == 0 else 1 + core],
            device_id=device(s, c), device_id_type=MESH,
        )

    across = rows_copy(0, 8 + core * HALF, 8 + core * HALF, HALF, other, col)
    target = col - 1 + 2 * core
    inside = jnp.logical_and(target >= 0, target < columns)
    borders = [rows_copy(1 + n, 8 + 24 * core, 40 - 40 * core, 8, 2 * z + n, target) for n in range(2)]

    @pl.when(inside)
    def _():
        for copy in borders:
            copy.start()

    across.start()

    blank = jnp.zeros((3, 8, LANES), F32)

    def border_wait(sender, first):
        pltpu.make_async_remote_copy(
            src_ref=image.at[:, pl.ds(first, 8)], dst_ref=image.at[:, pl.ds(first, 8)],
            send_sem=edge_send.at[0], recv_sem=edge_recv.at[1 + sender],
            device_id=device(slab, col), device_id_type=MESH,
        ).wait_recv()

    @pl.when(col == 0)
    def _():
        image[:, pl.ds(0, 8)] = blank

    @pl.when(col > 0)
    def _():
        border_wait(1, 0)

    @pl.when(col == columns - 1)
    def _():
        image[:, pl.ds(40, 8)] = blank

    @pl.when(col < columns - 1)
    def _():
        border_wait(0, 40)

    pltpu.make_async_remote_copy(
        src_ref=image.at[:, pl.ds(8, HALF)],
        dst_ref=image.at[:, pl.ds(pl.multiple_of(8 + (1 - core) * HALF, 8), HALF)],
        send_sem=edge_send.at[0], recv_sem=edge_recv.at[0],
        device_id=device(slab, col), device_id_type=MESH,
    ).wait_recv()

    image_out[...] = image[...]

    across.wait_send()

    @pl.when(inside)
    def _():
        for copy in borders:
            copy.wait_send()


def smooth_kernel(image, color_out, depth_out, coarse_out):
    core = lax.axis_index("slab") % 2
    for n, out in enumerate((color_out, depth_out, coarse_out)):
        smooth = 0.25 * image[n, pl.ds(7, 32)] + 0.5 * image[n, pl.ds(8, 32)] + 0.25 * image[n, pl.ds(9, 32)]
        turned = pltpu.roll(smooth, LANES // 2, 1)
        out[...] = jnp.where(core == 0, smooth, turned)[:, : LANES // 2]


def body(field, fine_plane, fine_frac, counts):
    channels, depth, rows, width = field.shape
    slots = fine_plane.shape[0]
    tiles = width // LANES
    dma = pltpu.SemaphoreType.DMA
    out = jax.ShapeDtypeStruct((rows, LANES // 2), F32)
    vmem = pl.BlockSpec(memory_space=pltpu.VMEM)
    anywhere = pl.BlockSpec(memory_space=pltpu.HBM)
    image = pl.pallas_call(
        kernel,
        out_shape=jax.ShapeDtypeStruct((3, rows + 16, LANES), F32),
        in_specs=[anywhere] * 4,
        out_specs=vmem,
        scratch_shapes=[
            pltpu.VMEM((channels, depth, rows, width), jnp.bfloat16),
            pltpu.VMEM((channels, rows, width), jnp.bfloat16),
            pltpu.VMEM((slots, rows, width), jnp.int32),
            pltpu.VMEM((slots, rows, width), jnp.int32),
            pltpu.VMEM((1, rows, width), jnp.int32),
            pltpu.VMEM((tiles, 5, HALF, LANES), F32),
            pltpu.VMEM((tiles, 5, HALF, LANES), F32),
            pltpu.VMEM((tiles, 5, HALF, LANES), F32),
            pltpu.VMEM((tiles, 5, 8, LANES), jnp.int32),
            pltpu.VMEM((tiles, 5, 8, LANES), jnp.int32),
            pltpu.VMEM((3, 48, LANES), F32),
            dma((4, tiles)),
            dma((tiles,)), dma((tiles,)),
            dma((tiles,)), dma((tiles,)),
            dma((tiles,)), dma((tiles,)),
            dma((3,)), dma((3,)),
            pltpu.SemaphoreType.REGULAR, pltpu.SemaphoreType.REGULAR,
        ],
        compiler_params=pltpu.CompilerParams(collective_id=0, has_side_effects=True, vmem_limit_bytes=56400000),
        name="render",
    )(field, fine_plane, fine_frac, counts)
    return pl.pallas_call(
        smooth_kernel,
        out_shape=(out, out, out),
        in_specs=[vmem],
        out_specs=(vmem, vmem, vmem),
        compiler_params=pltpu.CompilerParams(vmem_limit_bytes=4 << 20),
        name="smooth",
    )(image)


def solution(mesh):
    in_specs = (
        P(None, "slab", "col", None),
        P("slab", "col", None),
        P("slab", "col", None),
        P("slab", "col", None),
    )
    out_specs = (P("col", "slab"), P("col", "slab"), P("col", "slab"))
    return jax.shard_map(body, mesh=mesh, in_specs=in_specs, out_specs=out_specs, check_vma=False)
```

```python
import jax
import jax.numpy as jnp
from jax import lax
from jax.experimental import pallas as pl
from jax.experimental.pallas import tpu as pltpu
from jax.sharding import PartitionSpec as P

F32 = jnp.float32
MESH = pl.DeviceIdType.MESH
LANES = 128
HALF = 16
LOG2E = 1.4426950408889634
SHIFT = 0.5
TOP = 65535.0
COLOR_SPAN = (-22.5, 0.0)
DEPTH_SPAN = (-15.0, 10.75)


def pick(leaves, masks):
    for mask in masks:
        pairs = [jnp.where(mask, leaves[i + 1], leaves[i]) for i in range(0, len(leaves) - 1, 2)]
        leaves = pairs + leaves[2 * len(pairs) :]
    return leaves[0]


def softplus2(values):
    return jnp.log2(1.0 + jnp.exp2(values * LOG2E))


def march_group(field, halo, planes, fracs, counts, rows, cols, slab):
    depth = field.shape[1]
    slots = planes.shape[0]
    total = depth * 16
    scale = 2.0 / total

    def leaf(channel, plane):
        if plane == depth:
            return halo[channel, rows, cols]
        return field[channel, plane, rows, cols]

    shape = (HALF, LANES)
    live = counts[0, rows, cols]
    through, color, reach = jnp.ones(shape, F32), jnp.zeros(shape, F32), jnp.zeros(shape, F32)
    first = (slab * depth * 8).astype(F32) + SHIFT
    i16 = jnp.int16
    for slot in range(slots):
        plane = planes[slot, rows, cols]
        spot = (plane << 3) + fracs[slot, rows, cols]
        p = plane.astype(i16)
        up = p + i16(1)
        odd_bits = [(p & i16(2)) != i16(0), (p & i16(4)) != i16(0), p >= i16(8)]
        even_bits = [(up & i16(2)) != i16(0), (up & i16(4)) != i16(0), up >= i16(8), up >= i16(16)]
        even_weight = jnp.abs((spot & 15).astype(F32) * 0.125 - 1.0)
        values = []
        for channel in range(2):
            odd = pick([leaf(channel, k) for k in range(1, depth, 2)], odd_bits).astype(F32)
            even = pick([leaf(channel, k) for k in range(0, depth + 1, 2)], even_bits).astype(F32)
            values.append(odd + (even - odd) * even_weight)
        factor = jnp.exp2(softplus2(values[0]) * (-scale * depth / slots))
        after = through * jnp.where(live > slot, factor, 1.0)
        weight = through - after
        through = after
        color = color + weight * (1.0 + jnp.tanh(0.5 * values[1]))
        reach = reach + weight * (spot.astype(F32) + first)
    coarse_through, coarse = jnp.ones(shape, F32), jnp.zeros(shape, F32)
    for k in range(7, depth, 8):
        value, shine = [
            0.5 * (leaf(channel, k).astype(F32) + leaf(channel, k + 1).astype(F32)) for channel in range(2)
        ]
        after = coarse_through * jnp.exp2(softplus2(value) * (-8.0 * scale))
        coarse = coarse + (coarse_through - after) * (1.0 + jnp.tanh(0.5 * shine))
        coarse_through = after
    return 0.5 * color, reach, through, 0.5 * coarse, coarse_through


def as_code(u):
    return (jnp.clip(u, 0.0, TOP) + 0.5).astype(jnp.int32)


def encode_log(values, span):
    low, high = span
    step = TOP / (high - low)
    return as_code(jnp.log2(values) * step - low * step)


def decode_log(code, span):
    low, high = span
    return jnp.exp2(code.astype(F32) * ((high - low) / TOP) + low)


def kernel(
    field_in, plane_in, frac_in, count_in,
    image_out,
    field, front, halo, planes, fracs, counts, pool, packed, got, border, border_got,
    load_sem, halo_send, halo_recv, pair_send, pair_recv, chip_send, chip_recv, border_send, border_recv, behind, told,
):
    slab, col = lax.axis_index("slab"), lax.axis_index("col")
    slabs, columns = lax.axis_size("slab"), lax.axis_size("col")
    chips = slabs // 2
    z, core = slab // 2, slab % 2
    other = slab + 1 - 2 * core
    tiles = chips

    def device(s, c):
        return {"slab": s, "col": c}

    def lanes(tile):
        return pl.ds(pl.multiple_of(tile * LANES, LANES), LANES)

    def loads(i):
        cols = lanes(i)
        return [
            pltpu.make_async_copy(field_in.at[:, :, :, cols], field.at[:, :, :, cols], load_sem.at[0, i]),
            pltpu.make_async_copy(plane_in.at[:, :, cols], planes.at[:, :, cols], load_sem.at[1, i]),
            pltpu.make_async_copy(frac_in.at[:, :, cols], fracs.at[:, :, cols], load_sem.at[2, i]),
            pltpu.make_async_copy(count_in.at[:, :, cols], counts.at[:, :, cols], load_sem.at[3, i]),
        ]

    barrier = pltpu.get_barrier_semaphore()

    def tell(semaphore, s, c):
        pl.semaphore_signal(semaphore, inc=1, device_id=device(s, c), device_id_type=MESH)

    first_plane = pltpu.make_async_copy(field_in.at[:, 0], front, load_sem.at[0, tiles])

    @pl.when(slab > 0)
    def _():
        first_plane.start()

    tell(barrier, other, col)

    @pl.when(jnp.logical_and(core == 1, z < chips - 1))
    def _():
        tell(barrier, slab + 1, col)

    for copy in loads(0):
        copy.start()

    def tell_behind(chip, _):
        tell(barrier, 2 * chip + core, col)
        return 0

    lax.fori_loop(z + 1, chips, tell_behind, 0)

    def both_sides(act):
        @pl.when(col > 0)
        def _():
            act(0, col - 1)

        @pl.when(col < columns - 1)
        def _():
            act(1, col + 1)

    def greet_side(side, c):
        def tell_beside(chip, _):
            tell(barrier, 2 * chip + 1, c)
            return 0

        lax.fori_loop(z, chips, tell_beside, 0)

    both_sides(greet_side)

    def count(*conditions):
        return sum(jnp.where(c, 1, 0) for c in conditions)

    sides = count(col > 0, col < columns - 1)
    pl.semaphore_wait(barrier, 1 + z + (1 - core) * count(z > 0) + core * 2 * (z + 1) * sides)

    def front_copy(to, i):
        cols = lanes(i)
        return pltpu.make_async_remote_copy(
            src_ref=front.at[:, :, cols], dst_ref=halo.at[:, :, cols],
            send_sem=halo_send.at[i], recv_sem=halo_recv.at[i],
            device_id=device(to, col), device_id_type=MESH,
        )

    @pl.when(slab > 0)
    def _():
        first_plane.wait()

        def start_front(i, _):
            front_copy(slab - 1, i).start()
            return 0

        lax.fori_loop(0, tiles, start_front, 0)

    def told_ahead(chip, _):
        tell(behind, 2 * chip + core, col)
        return 0

    def aside(side, c):
        def told_aside(chip, _):
            tell(behind, 2 * chip + core, c)
            return 0

        lax.fori_loop(0, z, told_aside, 0)

    lax.fori_loop(0, z, told_ahead, 0)

    @pl.when(core == 1)
    def _():
        tell(told, other, col)
        both_sides(aside)

    def start_loads(i, _):
        for copy in loads(i):
            copy.start()
        return 0

    lax.fori_loop(1, tiles, start_loads, 0)

    @pl.when(slab == slabs - 1)
    def _():
        halo[...] = jnp.zeros_like(halo)

    @pl.when(core == 0)
    def _():
        pl.semaphore_wait(told, 1)
        both_sides(aside)

    def pair_copy(i):
        return pltpu.make_async_remote_copy(
            src_ref=pool.at[i, 2], dst_ref=pool.at[i, core],
            send_sem=pair_send.at[i], recv_sem=pair_recv.at[i],
            device_id=device(other, col), device_id_type=MESH,
        )

    def chip_copy(i):
        return pltpu.make_async_remote_copy(
            src_ref=packed.at[i], dst_ref=got.at[z],
            send_sem=chip_send.at[i], recv_sem=chip_recv.at[z],
            device_id=device(2 * i + core, col), device_id_type=MESH,
        )

    def border_copy(i, side, c):
        return pltpu.make_async_remote_copy(
            src_ref=border.at[i], dst_ref=border_got.at[1 - side, z],
            send_sem=border_send.at[side, i], recv_sem=border_recv.at[1 - side, z],
            device_id=device(2 * i + core, c), device_id_type=MESH,
        )

    left = lax.broadcasted_iota(jnp.int32, (8, LANES), 1) < LANES // 2
    left_slot = jnp.where(core == 0, 0, 2)
    right_slot = jnp.where(core == 0, 2, 1)

    def march(i):
        for copy in loads(i):
            copy.wait()

        @pl.when(slab < slabs - 1)
        def _():
            front_copy(slab, i).wait_recv()

        parts = [
            march_group(field, halo, planes, fracs, counts, pl.ds(HALF * g, HALF), lanes(i), slab) for g in range(2)
        ]
        for n, (upper, lower) in enumerate(zip(*parts)):
            for m in range(2):
                up, down = upper[8 * m : 8 * m + 8], lower[8 * m : 8 * m + 8]
                pool[i, left_slot, n, pl.ds(8 * m, 8)] = jnp.where(left, up, pltpu.roll(down, LANES // 2, 1))
                pool[i, right_slot, n, pl.ds(8 * m, 8)] = jnp.where(left, pltpu.roll(up, LANES // 2, 1), down)
        pair_copy(i).start()

    def join(i):
        pair_copy(i).wait_recv()
        halves, edges = [], []
        for m in range(2):
            front = [pool[i, 0, n, pl.ds(8 * m, 8)] for n in range(5)]
            back = [pool[i, 1, n, pl.ds(8 * m, 8)] for n in range(5)]
            color = front[0] + front[2] * back[0]
            reach = front[1] + front[2] * back[1]
            coarse = front[3] + front[4] * back[3]
            fine, plain = front[2] * back[2], front[4] * back[4]
            halves.append([
                encode_log(color, COLOR_SPAN), encode_log(reach, DEPTH_SPAN), as_code(fine * TOP),
                encode_log(coarse, COLOR_SPAN), as_code(plain * TOP),
            ])
            edges.append([color, reach, fine, coarse, plain])
        for n, (first, last) in enumerate(zip(*edges)):
            border[i, pl.ds(n, 1)] = jnp.where(left[:1], first[:1], last[7:])
        words = [first | (last << 16) for first, last in zip(*halves)]

        @pl.when(i == z)
        def _():
            for n, word in enumerate(words):
                got[z, n] = word

        @pl.when(i != z)
        def _():
            for n, word in enumerate(words):
                packed[i, n] = word

    def send(i):
        @pl.when(i != z)
        def _():
            chip_copy(i).start()

        both_sides(lambda side, c: border_copy(i, side, c).start())

    def finish(i):
        join(i)

        @pl.when(i <= z)
        def _():
            send(i)

    def step(i, _):
        march(i)
        finish(i - 1)
        return 0

    march(0)
    lax.fori_loop(1, tiles, step, 0)
    finish(tiles - 1)

    @pl.when(z < chips - 1)
    def _():
        pl.semaphore_wait(behind, (chips - 1 - z) * (1 + sides))

        def send_behind(i, _):
            send(i)
            return 0

        lax.fori_loop(z + 1, chips, send_behind, 0)

    @pl.when(slab > 0)
    def _():
        def end_front(i, _):
            front_copy(slab - 1, i).wait_send()
            return 0

        lax.fori_loop(0, tiles, end_front, 0)

    def end_tile(i, _):
        pair_copy(i).wait_send()

        @pl.when(i != z)
        def _():
            chip_copy(i).wait_send()

        both_sides(lambda side, c: border_copy(i, side, c).wait_send())
        return 0

    lax.fori_loop(0, tiles, end_tile, 0)

    shape = (8, LANES)
    state = [[jnp.ones(shape, F32), jnp.ones(shape, F32)] + [jnp.zeros(shape, F32)] * 3 for _ in range(2)]
    for chip in range(chips):

        @pl.when(z != chip)
        def _():
            pltpu.make_async_remote_copy(
                src_ref=packed.at[0], dst_ref=got.at[chip], send_sem=chip_send.at[0], recv_sem=chip_recv.at[chip],
                device_id=device(slab, col), device_id_type=MESH,
            ).wait_recv()

        words = [got[chip, n] for n in range(5)]
        for half in range(2):
            codes = [(w & 0xFFFF) if half == 0 else (lax.shift_right_logical(w, 16)) for w in words]
            fine, plain, color, reach, coarse = state[half]
            color = color + fine * decode_log(codes[0], COLOR_SPAN)
            reach = reach + fine * decode_log(codes[1], DEPTH_SPAN)
            coarse = coarse + plain * decode_log(codes[3], COLOR_SPAN)
            fine = fine * (codes[2].astype(F32) * (1.0 / TOP))
            plain = plain * (codes[4].astype(F32) * (1.0 / TOP))
            state[half] = [fine, plain, color, reach, coarse]
    for half in range(2):
        fine, plain, color, reach, coarse = state[half]
        rows = pl.ds(8 * half, 8)
        image_out[0, rows] = color
        image_out[1, rows] = (reach - SHIFT * (1.0 - fine)) * (1.0 / 2048)
        image_out[2, rows] = coarse

    def border_waits(side, c):
        for chip in range(chips):
            pltpu.make_async_remote_copy(
                src_ref=border.at[0], dst_ref=border_got.at[side, chip],
                send_sem=border_send.at[side, 0], recv_sem=border_recv.at[side, chip],
                device_id=device(slab, c), device_id_type=MESH,
            ).wait_recv()

    both_sides(border_waits)
    line = (1, LANES)
    fine, plain = jnp.ones(line, F32), jnp.ones(line, F32)
    color, reach, coarse = [jnp.zeros(line, F32)] * 3
    for chip in range(chips):
        parts = [
            jnp.where(left[:1], border_got[1, chip, pl.ds(n, 1)], border_got[0, chip, pl.ds(n, 1)]) for n in range(5)
        ]
        color, reach, coarse = color + fine * parts[0], reach + fine * parts[1], coarse + plain * parts[3]
        fine, plain = fine * parts[2], plain * parts[4]
    there = jnp.where(left, jnp.where(col < columns - 1, 1.0, 0.0), jnp.where(col > 0, 1.0, 0.0))
    for n, row in enumerate((color, (reach - SHIFT * (1.0 - fine)) * (1.0 / 2048), coarse)):
        row = jnp.where(there > 0.5, jnp.broadcast_to(row, (8, LANES)), 0.0)
        image_out[n, pl.ds(2 * 8, 8)] = pltpu.roll(row, LANES // 2, 1)


def smooth_kernel(image, color_out, depth_out, coarse_out, padded):
    half = LANES // 2
    for n, out in enumerate((color_out, depth_out, coarse_out)):
        whole = image[n]
        turned = pltpu.roll(whole, half, 1)
        padded[n, pl.ds(7, 1)] = whole[16:17]
        padded[n, pl.ds(8, HALF)] = whole[:HALF]
        padded[n, pl.ds(8 + HALF, HALF)] = turned[:HALF]
        padded[n, pl.ds(8 + 2 * HALF, 1)] = turned[16:17]
        smooth = 0.25 * padded[n, pl.ds(7, 32)] + 0.5 * padded[n, pl.ds(8, 32)] + 0.25 * padded[n, pl.ds(9, 32)]
        out[...] = smooth[:, :half]


def body(field, fine_plane, fine_frac, counts):
    channels, depth, rows, width = field.shape
    slots = fine_plane.shape[0]
    tiles = width // LANES
    dma = pltpu.SemaphoreType.DMA
    out = jax.ShapeDtypeStruct((rows, LANES // 2), F32)
    vmem = pl.BlockSpec(memory_space=pltpu.VMEM)
    anywhere = pl.BlockSpec(memory_space=pltpu.HBM)
    image = pl.pallas_call(
        kernel,
        out_shape=jax.ShapeDtypeStruct((3, 24, LANES), F32),
        in_specs=[anywhere] * 4,
        out_specs=vmem,
        scratch_shapes=[
            pltpu.VMEM((channels, depth, rows, width), jnp.bfloat16),
            pltpu.VMEM((channels, rows, width), jnp.bfloat16),
            pltpu.VMEM((channels, rows, width), jnp.bfloat16),
            pltpu.VMEM((slots, rows, width), jnp.int32),
            pltpu.VMEM((slots, rows, width), jnp.int32),
            pltpu.VMEM((1, rows, width), jnp.int32),
            pltpu.VMEM((tiles, 3, 5, HALF, LANES), F32),
            pltpu.VMEM((tiles, 5, 8, LANES), jnp.int32),
            pltpu.VMEM((tiles, 5, 8, LANES), jnp.int32),
            pltpu.VMEM((tiles, 8, LANES), F32),
            pltpu.VMEM((2, tiles, 8, LANES), F32),
            dma((4, tiles + 1)),
            dma((tiles,)), dma((tiles,)),
            dma((tiles,)), dma((tiles,)),
            dma((tiles,)), dma((tiles,)),
            dma((2, tiles)), dma((2, tiles)),
            pltpu.SemaphoreType.REGULAR, pltpu.SemaphoreType.REGULAR,
        ],
        compiler_params=pltpu.CompilerParams(collective_id=0, has_side_effects=True, vmem_limit_bytes=56400000),
        name="render",
    )(field, fine_plane, fine_frac, counts)
    return pl.pallas_call(
        smooth_kernel,
        out_shape=(out, out, out),
        in_specs=[vmem],
        out_specs=(vmem, vmem, vmem),
        scratch_shapes=[pltpu.VMEM((3, rows + 16, LANES), F32)],
        compiler_params=pltpu.CompilerParams(vmem_limit_bytes=4 << 20),
        name="smooth",
    )(image)


def solution(mesh):
    in_specs = (
        P(None, "slab", "col", None),
        P("slab", "col", None),
        P("slab", "col", None),
        P("slab", "col", None),
    )
    out_specs = (P("col", "slab"), P("col", "slab"), P("col", "slab"))
    return jax.shard_map(body, mesh=mesh, in_specs=in_specs, out_specs=out_specs, check_vma=False)
```

```python
import jax
import jax.numpy as jnp
from jax import lax
from jax.experimental import pallas as pl
from jax.experimental.pallas import tpu as pltpu
from jax.sharding import PartitionSpec as P

F32 = jnp.float32
MESH = pl.DeviceIdType.MESH
LANES = 128
LEADERS = 3
HALF = 16
LOG2E = 1.4426950408889634
SHIFT = 0.5
TOP = 65535.0
COLOR_SPAN = (-22.5, 0.0)
DEPTH_SPAN = (-15.0, 10.75)


def pick(leaves, masks):
    for mask in masks:
        pairs = [jnp.where(mask, leaves[i + 1], leaves[i]) for i in range(0, len(leaves) - 1, 2)]
        leaves = pairs + leaves[2 * len(pairs) :]
    return leaves[0]


def softplus2(values):
    return jnp.log2(1.0 + jnp.exp2(values * LOG2E))


def march_group(field, halo, planes, fracs, counts, rows, cols, slab):
    depth = field.shape[1]
    slots = planes.shape[0]
    total = depth * 16
    scale = 2.0 / total

    def leaf(channel, plane):
        if plane == depth:
            return halo[channel, rows, cols]
        return field[channel, plane, rows, cols]

    shape = (HALF, LANES)
    live = counts[0, rows, cols]
    through, color, reach = jnp.ones(shape, F32), jnp.zeros(shape, F32), jnp.zeros(shape, F32)
    first = (slab * depth * 8).astype(F32) + SHIFT
    i16 = jnp.int16
    for slot in range(slots):
        plane = planes[slot, rows, cols]
        spot = (plane << 3) + fracs[slot, rows, cols]
        p = plane.astype(i16)
        up = p + i16(1)
        odd_bits = [(p & i16(2)) != i16(0), (p & i16(4)) != i16(0), p >= i16(8)]
        even_bits = [(up & i16(2)) != i16(0), (up & i16(4)) != i16(0), up >= i16(8), up >= i16(16)]
        even_weight = jnp.abs((spot & 15).astype(F32) * 0.125 - 1.0)
        values = []
        for channel in range(2):
            odd = pick([leaf(channel, k) for k in range(1, depth, 2)], odd_bits).astype(F32)
            even = pick([leaf(channel, k) for k in range(0, depth + 1, 2)], even_bits).astype(F32)
            values.append(odd + (even - odd) * even_weight)
        factor = jnp.exp2(softplus2(values[0]) * (-scale * depth / slots))
        after = through * jnp.where(live > slot, factor, 1.0)
        weight = through - after
        through = after
        color = color + weight * (1.0 + jnp.tanh(0.5 * values[1]))
        reach = reach + weight * (spot.astype(F32) + first)
    coarse_through, coarse = jnp.ones(shape, F32), jnp.zeros(shape, F32)
    for k in range(7, depth, 8):
        value, shine = [
            0.5 * (leaf(channel, k).astype(F32) + leaf(channel, k + 1).astype(F32)) for channel in range(2)
        ]
        after = coarse_through * jnp.exp2(softplus2(value) * (-8.0 * scale))
        coarse = coarse + (coarse_through - after) * (1.0 + jnp.tanh(0.5 * shine))
        coarse_through = after
    return 0.5 * color, reach, through, 0.5 * coarse, coarse_through


def as_code(u):
    return (jnp.clip(u, 0.0, TOP) + 0.5).astype(jnp.int32)


def encode_log(values, span):
    low, high = span
    step = TOP / (high - low)
    return as_code(jnp.log2(values) * step - low * step)


def decode_log(code, span):
    low, high = span
    return jnp.exp2(code.astype(F32) * ((high - low) / TOP) + low)


def kernel(
    field_in, plane_in, frac_in, count_in,
    image_out,
    field, front, halo, planes, fracs, counts, pool, packed, got, border, border_got,
    load_sem, halo_send, halo_recv, pair_send, pair_recv, chip_send, chip_recv, border_send, border_recv, behind, level, told,
):
    slab, col = lax.axis_index("slab"), lax.axis_index("col")
    slabs, columns = lax.axis_size("slab"), lax.axis_size("col")
    chips = slabs // 2
    z, core = slab // 2, slab % 2
    other = slab + 1 - 2 * core
    tiles = chips

    def device(s, c):
        return {"slab": s, "col": c}

    def lanes(tile):
        return pl.ds(pl.multiple_of(tile * LANES, LANES), LANES)

    spans = [(0, 1), (1, tiles // 2), (tiles // 2, tiles)]

    def span(first, last):
        return pl.ds(first * LANES, (last - first) * LANES)

    def loads(n, cols):
        return [
            pltpu.make_async_copy(field_in.at[:, :, :, cols], field.at[:, :, :, cols], load_sem.at[0, n]),
            pltpu.make_async_copy(plane_in.at[:, :, cols], planes.at[:, :, cols], load_sem.at[1, n]),
            pltpu.make_async_copy(frac_in.at[:, :, cols], fracs.at[:, :, cols], load_sem.at[2, n]),
            pltpu.make_async_copy(count_in.at[:, :, cols], counts.at[:, :, cols], load_sem.at[3, n]),
        ]

    first_load, other_load = loads(0, span(0, 1)), loads(1, span(1, tiles))

    barrier = pltpu.get_barrier_semaphore()

    def tell(semaphore, s, c):
        pl.semaphore_signal(semaphore, inc=1, device_id=device(s, c), device_id_type=MESH)

    first_plane = [
        pltpu.make_async_copy(field_in.at[:, 0, :, cols], front.at[:, :, cols], load_sem.at[4, n])
        for n, cols in enumerate((span(0, 1), span(1, tiles)))
    ]

    @pl.when(slab > 0)
    def _():
        for copy in first_plane:
            copy.start()

    tell(barrier, other, col)

    @pl.when(jnp.logical_and(core == 1, z < chips - 1))
    def _():
        tell(barrier, slab + 1, col)

    for copy in first_load:
        copy.start()

    def tell_behind(chip, _):
        tell(barrier, 2 * chip + 1, col)
        return 0

    lax.fori_loop(z + 1, chips, tell_behind, 0)

    def both_sides(act):
        @pl.when(col > 0)
        def _():
            act(0, col - 1)

        @pl.when(col < columns - 1)
        def _():
            act(1, col + 1)

    def greet_side(side, c):
        def tell_beside(chip, _):
            tell(barrier, 2 * chip + 1, c)
            return 0

        lax.fori_loop(jnp.where(z == 0, 0, jnp.where(z < LEADERS, z + 1, chips)), chips, tell_beside, 0)

    both_sides(greet_side)

    for copy in other_load:
        copy.start()

    def count(*conditions):
        return sum(jnp.where(c, 1, 0) for c in conditions)

    sides = count(col > 0, col < columns - 1)
    pl.semaphore_wait(barrier, 1 + jnp.where(core == 1, 2 * z + 2 * jnp.clip(z, 1, LEADERS) * sides, count(z > 0)))

    def front_copy(to, n):
        cols = span(*spans[n])
        return pltpu.make_async_remote_copy(
            src_ref=front.at[:, :, cols], dst_ref=halo.at[:, :, cols],
            send_sem=halo_send, recv_sem=halo_recv.at[n],
            device_id=device(to, col), device_id_type=MESH,
        )

    @pl.when(slab > 0)
    def _():
        first_plane[0].wait()
        front_copy(slab - 1, 0).start()
        first_plane[1].wait()
        for n in range(1, len(spans)):
            front_copy(slab - 1, n).start()

    def told_ahead(chip, _):
        tell(behind, 2 * chip + core, col)
        return 0

    def aside(side, c):
        @pl.when(z > 0)
        def _():
            tell(behind, core, c)

    @pl.when(core == 1)
    def _():
        tell(told, other, col)
        lax.fori_loop(0, z, told_ahead, 0)
        both_sides(aside)

    @pl.when(slab == slabs - 1)
    def _():
        halo[...] = jnp.zeros_like(halo)

    @pl.when(core == 0)
    def _():
        pl.semaphore_wait(told, 1)
        lax.fori_loop(0, z, told_ahead, 0)
        both_sides(aside)

    def pair_copy(i):
        return pltpu.make_async_remote_copy(
            src_ref=pool.at[i, 2], dst_ref=pool.at[i, core],
            send_sem=pair_send, recv_sem=pair_recv.at[i],
            device_id=device(other, col), device_id_type=MESH,
        )

    def chip_copy(i):
        return pltpu.make_async_remote_copy(
            src_ref=packed.at[i], dst_ref=got.at[z],
            send_sem=chip_send, recv_sem=chip_recv.at[z],
            device_id=device(2 * i + core, col), device_id_type=MESH,
        )

    def border_copy(i, side, c):
        return pltpu.make_async_remote_copy(
            src_ref=border.at[i], dst_ref=border_got.at[1 - side, z],
            send_sem=border_send.at[side], recv_sem=border_recv.at[1 - side],
            device_id=device(2 * i + core, c), device_id_type=MESH,
        )

    left = lax.broadcasted_iota(jnp.int32, (8, LANES), 1) < LANES // 2
    left_slot = jnp.where(core == 0, 0, 2)
    right_slot = jnp.where(core == 0, 2, 1)

    def hear_front(n):
        @pl.when(slab < slabs - 1)
        def _():
            front_copy(slab, n).wait_recv()

    def march(i):
        parts = [
            march_group(field, halo, planes, fracs, counts, pl.ds(HALF * g, HALF), lanes(i), slab) for g in range(2)
        ]
        for n, (upper, lower) in enumerate(zip(*parts)):
            for m in range(2):
                up, down = upper[8 * m : 8 * m + 8], lower[8 * m : 8 * m + 8]
                pool[i, left_slot, n, pl.ds(8 * m, 8)] = jnp.where(left, up, pltpu.roll(down, LANES // 2, 1))
                pool[i, right_slot, n, pl.ds(8 * m, 8)] = jnp.where(left, pltpu.roll(up, LANES // 2, 1), down)
        pair_copy(i).start()

    def join(i):
        pair_copy(i).wait_recv()
        halves, edges = [], []
        for m in range(2):
            front = [pool[i, 0, n, pl.ds(8 * m, 8)] for n in range(5)]
            back = [pool[i, 1, n, pl.ds(8 * m, 8)] for n in range(5)]
            color = front[0] + front[2] * back[0]
            reach = front[1] + front[2] * back[1]
            coarse = front[3] + front[4] * back[3]
            fine, plain = front[2] * back[2], front[4] * back[4]
            halves.append([
                encode_log(color, COLOR_SPAN), encode_log(reach, DEPTH_SPAN), as_code(fine * TOP),
                encode_log(coarse, COLOR_SPAN), as_code(plain * TOP),
            ])
            edges.append([color, reach, fine, coarse, plain])
        for n, (first, last) in enumerate(zip(*edges)):
            border[i, pl.ds(n, 1)] = jnp.where(left[:1], first[:1], last[7:])
        words = [first | (last << 16) for first, last in zip(*halves)]

        @pl.when(i == z)
        def _():
            for n, word in enumerate(words):
                got[z, n] = word

        @pl.when(i != z)
        def _():
            for n, word in enumerate(words):
                packed[i, n] = word

    def send_border(i):
        both_sides(lambda side, c: border_copy(i, side, c).start())

    def finish(i):
        join(i)

        @pl.when(i < z)
        def _():
            chip_copy(i).start()

        @pl.when(i < jnp.minimum(z, LEADERS))
        def _():
            send_border(i)

    def step(i, _):
        @pl.when(i == tiles // 2)
        def _():
            hear_front(2)

        march(i)
        finish(i - 1)
        return 0

    for copy in first_load:
        copy.wait()
    hear_front(0)
    march(0)
    finish(0)
    for copy in other_load:
        copy.wait()
    hear_front(1)
    march(1)
    lax.fori_loop(2, tiles, step, 0)
    finish(tiles - 1)

    @pl.when(z < chips - 1)
    def _():
        pl.semaphore_wait(behind, (chips - 1 - z) * jnp.where(z == 0, 1 + sides, 1))

    @pl.when(z == 0)
    def _():
        def tell_level(chip, _):
            tell(level, 2 * chip + core, col)
            return 0

        lax.fori_loop(1, chips, tell_level, 0)

    def send_behind(i, _):
        chip_copy(i).start()
        return 0

    lax.fori_loop(z + 1, chips, send_behind, 0)

    @pl.when(z > 0)
    def _():
        pl.semaphore_wait(level, 1)

    def send_beside(i, _):
        send_border(i)
        return 0

    lax.fori_loop(jnp.minimum(z, LEADERS), chips, send_beside, 0)

    shape = (8, LANES)
    state = [[jnp.ones(shape, F32), jnp.ones(shape, F32)] + [jnp.zeros(shape, F32)] * 3 for _ in range(2)]
    for chip in range(chips):

        @pl.when(z != chip)
        def _():
            pltpu.make_async_remote_copy(
                src_ref=packed.at[0], dst_ref=got.at[chip], send_sem=chip_send, recv_sem=chip_recv.at[chip],
                device_id=device(slab, col), device_id_type=MESH,
            ).wait_recv()

        words = [got[chip, n] for n in range(5)]
        for half in range(2):
            codes = [(w & 0xFFFF) if half == 0 else (lax.shift_right_logical(w, 16)) for w in words]
            fine, plain, color, reach, coarse = state[half]
            color = color + fine * decode_log(codes[0], COLOR_SPAN)
            reach = reach + fine * decode_log(codes[1], DEPTH_SPAN)
            coarse = coarse + plain * decode_log(codes[3], COLOR_SPAN)
            fine = fine * (codes[2].astype(F32) * (1.0 / TOP))
            plain = plain * (codes[4].astype(F32) * (1.0 / TOP))
            state[half] = [fine, plain, color, reach, coarse]
    for half in range(2):
        fine, plain, color, reach, coarse = state[half]
        rows = pl.ds(8 * half, 8)
        image_out[0, rows] = color
        image_out[1, rows] = (reach - SHIFT * (1.0 - fine)) * (1.0 / 2048)
        image_out[2, rows] = coarse

    def all_borders(side, c):
        return pltpu.make_async_remote_copy(
            src_ref=border, dst_ref=border_got.at[side], send_sem=border_send.at[side], recv_sem=border_recv.at[side],
            device_id=device(slab, c), device_id_type=MESH,
        )

    both_sides(lambda side, c: all_borders(side, c).wait_recv())
    line = (1, LANES)
    fine, plain = jnp.ones(line, F32), jnp.ones(line, F32)
    color, reach, coarse = [jnp.zeros(line, F32)] * 3
    for chip in range(chips):
        parts = [
            jnp.where(left[:1], border_got[1, chip, pl.ds(n, 1)], border_got[0, chip, pl.ds(n, 1)]) for n in range(5)
        ]
        color, reach, coarse = color + fine * parts[0], reach + fine * parts[1], coarse + plain * parts[3]
        fine, plain = fine * parts[2], plain * parts[4]
    there = jnp.where(left, jnp.where(col < columns - 1, 1.0, 0.0), jnp.where(col > 0, 1.0, 0.0))
    for n, row in enumerate((color, (reach - SHIFT * (1.0 - fine)) * (1.0 / 2048), coarse)):
        row = jnp.where(there > 0.5, jnp.broadcast_to(row, (8, LANES)), 0.0)
        image_out[n, pl.ds(2 * 8, 8)] = pltpu.roll(row, LANES // 2, 1)

    @pl.when(slab > 0)
    def _():
        pltpu.make_async_remote_copy(
            src_ref=front, dst_ref=halo, send_sem=halo_send, recv_sem=halo_recv.at[0],
            device_id=device(slab - 1, col), device_id_type=MESH,
        ).wait_send()

    pltpu.make_async_remote_copy(
        src_ref=pool.at[:, 2], dst_ref=pool.at[:, core], send_sem=pair_send, recv_sem=pair_recv.at[0],
        device_id=device(other, col), device_id_type=MESH,
    ).wait_send()
    others = pl.ds(0, tiles - 1)
    pltpu.make_async_remote_copy(
        src_ref=packed.at[others], dst_ref=got.at[others], send_sem=chip_send, recv_sem=chip_recv.at[0],
        device_id=device(other, col), device_id_type=MESH,
    ).wait_send()
    both_sides(lambda side, c: all_borders(side, c).wait_send())


def smooth_kernel(image, color_out, depth_out, coarse_out, padded):
    half = LANES // 2
    for n, out in enumerate((color_out, depth_out, coarse_out)):
        whole = image[n]
        turned = pltpu.roll(whole, half, 1)
        padded[n, pl.ds(7, 1)] = whole[16:17]
        padded[n, pl.ds(8, HALF)] = whole[:HALF]
        padded[n, pl.ds(8 + HALF, HALF)] = turned[:HALF]
        padded[n, pl.ds(8 + 2 * HALF, 1)] = turned[16:17]
        smooth = 0.25 * padded[n, pl.ds(7, 32)] + 0.5 * padded[n, pl.ds(8, 32)] + 0.25 * padded[n, pl.ds(9, 32)]
        out[...] = smooth[:, :half]


def body(field, fine_plane, fine_frac, counts):
    channels, depth, rows, width = field.shape
    slots = fine_plane.shape[0]
    tiles = width // LANES
    dma = pltpu.SemaphoreType.DMA
    out = jax.ShapeDtypeStruct((rows, LANES // 2), F32)
    vmem = pl.BlockSpec(memory_space=pltpu.VMEM)
    anywhere = pl.BlockSpec(memory_space=pltpu.HBM)
    image = pl.pallas_call(
        kernel,
        out_shape=jax.ShapeDtypeStruct((3, 24, LANES), F32),
        in_specs=[anywhere] * 4,
        out_specs=vmem,
        scratch_shapes=[
            pltpu.VMEM((channels, depth, rows, width), jnp.bfloat16),
            pltpu.VMEM((channels, rows, width), jnp.bfloat16),
            pltpu.VMEM((channels, rows, width), jnp.bfloat16),
            pltpu.VMEM((slots, rows, width), jnp.int32),
            pltpu.VMEM((slots, rows, width), jnp.int32),
            pltpu.VMEM((1, rows, width), jnp.int32),
            pltpu.VMEM((tiles, 3, 5, HALF, LANES), F32),
            pltpu.VMEM((tiles, 5, 8, LANES), jnp.int32),
            pltpu.VMEM((tiles, 5, 8, LANES), jnp.int32),
            pltpu.VMEM((tiles, 8, LANES), F32),
            pltpu.VMEM((2, tiles, 8, LANES), F32),
            dma((5, 2)),
            dma, dma((3,)),
            dma, dma((tiles,)),
            dma, dma((tiles,)),
            dma((2,)), dma((2,)),
            pltpu.SemaphoreType.REGULAR, pltpu.SemaphoreType.REGULAR, pltpu.SemaphoreType.REGULAR,
        ],
        compiler_params=pltpu.CompilerParams(collective_id=0, has_side_effects=True, vmem_limit_bytes=56400000),
        name="render",
    )(field, fine_plane, fine_frac, counts)
    return pl.pallas_call(
        smooth_kernel,
        out_shape=(out, out, out),
        in_specs=[vmem],
        out_specs=(vmem, vmem, vmem),
        scratch_shapes=[pltpu.VMEM((3, rows + 16, LANES), F32)],
        compiler_params=pltpu.CompilerParams(vmem_limit_bytes=4 << 20),
        name="smooth",
    )(image)


def solution(mesh):
    in_specs = (
        P(None, "slab", "col", None),
        P("slab", "col", None),
        P("slab", "col", None),
        P("slab", "col", None),
    )
    out_specs = (P("col", "slab"), P("col", "slab"), P("col", "slab"))
    return jax.shard_map(body, mesh=mesh, in_specs=in_specs, out_specs=out_specs, check_vma=False)
```

```python
import jax
import jax.numpy as jnp
from jax import lax
from jax.experimental import pallas as pl
from jax.experimental.pallas import tpu as pltpu
from jax.sharding import PartitionSpec as P

F32 = jnp.float32
MESH = pl.DeviceIdType.MESH
LANES = 128
AHEAD = 5
LEADERS = 4
HALF = 16
LOG2E = 1.4426950408889634
SHIFT = 0.5
TOP = 65535.0
COLOR_SPAN = (-22.5, 0.0)
DEPTH_SPAN = (-15.0, 10.75)


def pick(leaves, masks):
    for mask in masks:
        pairs = [jnp.where(mask, leaves[i + 1], leaves[i]) for i in range(0, len(leaves) - 1, 2)]
        leaves = pairs + leaves[2 * len(pairs) :]
    return leaves[0]


def softplus2(values):
    return jnp.log2(1.0 + jnp.exp2(values * LOG2E))


def march_group(field, halo, planes, fracs, counts, rows, cols, slab):
    depth = field.shape[1]
    slots = planes.shape[0]
    total = depth * 16
    scale = 2.0 / total

    def leaf(channel, plane):
        if plane == depth:
            return halo[channel, rows, cols]
        return field[channel, plane, rows, cols]

    shape = (HALF, LANES)
    live = counts[0, rows, cols]
    through, color, reach = jnp.ones(shape, F32), jnp.zeros(shape, F32), jnp.zeros(shape, F32)
    first = (slab * depth * 8).astype(F32) + SHIFT
    i16 = jnp.int16
    for slot in range(slots):
        plane = planes[slot, rows, cols]
        spot = (plane << 3) + fracs[slot, rows, cols]
        p = plane.astype(i16)
        up = p + i16(1)
        odd_bits = [(p & i16(2)) != i16(0), (p & i16(4)) != i16(0), p >= i16(8)]
        even_bits = [(up & i16(2)) != i16(0), (up & i16(4)) != i16(0), up >= i16(8), up >= i16(16)]
        even_weight = jnp.abs((spot & 15).astype(F32) * 0.125 - 1.0)
        values = []
        for channel in range(2):
            odd = pick([leaf(channel, k) for k in range(1, depth, 2)], odd_bits).astype(F32)
            even = pick([leaf(channel, k) for k in range(0, depth + 1, 2)], even_bits).astype(F32)
            values.append(odd + (even - odd) * even_weight)
        factor = jnp.exp2(softplus2(values[0]) * (-scale * depth / slots))
        after = through * jnp.where(live > slot, factor, 1.0)
        weight = through - after
        through = after
        color = color + weight * (1.0 + jnp.tanh(0.5 * values[1]))
        reach = reach + weight * (spot.astype(F32) + first)
    coarse_through, coarse = jnp.ones(shape, F32), jnp.zeros(shape, F32)
    for k in range(7, depth, 8):
        value, shine = [
            0.5 * (leaf(channel, k).astype(F32) + leaf(channel, k + 1).astype(F32)) for channel in range(2)
        ]
        after = coarse_through * jnp.exp2(softplus2(value) * (-8.0 * scale))
        coarse = coarse + (coarse_through - after) * (1.0 + jnp.tanh(0.5 * shine))
        coarse_through = after
    return 0.5 * color, reach, through, 0.5 * coarse, coarse_through


def as_code(u):
    return (jnp.clip(u, 0.0, TOP) + 0.5).astype(jnp.int32)


def encode_log(values, span):
    low, high = span
    step = TOP / (high - low)
    return as_code(jnp.log2(values) * step - low * step)


def decode_log(code, span):
    low, high = span
    return jnp.exp2(code.astype(F32) * ((high - low) / TOP) + low)


def kernel(
    field_in, plane_in, frac_in, count_in,
    image_out,
    field, front, halo, planes, fracs, counts, pool, packed, got, border, border_got,
    load_sem, halo_send, halo_recv, pair_send, pair_recv, chip_send, chip_recv, border_send, border_recv, behind, level, told,
):
    slab, col = lax.axis_index("slab"), lax.axis_index("col")
    slabs, columns = lax.axis_size("slab"), lax.axis_size("col")
    chips = slabs // 2
    z, core = slab // 2, slab % 2
    other = slab + 1 - 2 * core
    tiles = chips

    def device(s, c):
        return {"slab": s, "col": c}

    def lanes(tile):
        return pl.ds(pl.multiple_of(tile * LANES, LANES), LANES)

    spans = [(0, 1), (1, tiles // 2), (tiles // 2, tiles)]

    def span(first, last):
        return pl.ds(first * LANES, (last - first) * LANES)

    def loads(n, cols):
        return [
            pltpu.make_async_copy(field_in.at[:, :, :, cols], field.at[:, :, :, cols], load_sem.at[0, n]),
            pltpu.make_async_copy(plane_in.at[:, :, cols], planes.at[:, :, cols], load_sem.at[1, n]),
            pltpu.make_async_copy(frac_in.at[:, :, cols], fracs.at[:, :, cols], load_sem.at[2, n]),
            pltpu.make_async_copy(count_in.at[:, :, cols], counts.at[:, :, cols], load_sem.at[3, n]),
        ]

    first_load, other_load = loads(0, span(0, 1)), loads(1, span(1, tiles))

    barrier = pltpu.get_barrier_semaphore()

    def tell(semaphore, s, c):
        pl.semaphore_signal(semaphore, inc=1, device_id=device(s, c), device_id_type=MESH)

    first_plane = [
        pltpu.make_async_copy(field_in.at[:, 0, :, cols], front.at[:, :, cols], load_sem.at[4, n])
        for n, cols in enumerate((span(0, 1), span(1, tiles)))
    ]

    @pl.when(slab > 0)
    def _():
        for copy in first_plane:
            copy.start()

    tell(barrier, other, col)

    @pl.when(jnp.logical_and(core == 1, z < chips - 1))
    def _():
        tell(barrier, slab + 1, col)

    for copy in first_load:
        copy.start()

    def tell_behind(chip, _):
        tell(barrier, 2 * chip + 1, col)
        return 0

    lax.fori_loop(z + 1, chips, tell_behind, 0)

    def both_sides(act):
        @pl.when(col > 0)
        def _():
            act(0, col - 1)

        @pl.when(col < columns - 1)
        def _():
            act(1, col + 1)

    def greet_side(side, c):
        def tell_beside(chip, _):
            tell(barrier, 2 * chip + 1, c)
            return 0

        lax.fori_loop(jnp.where(z < LEADERS, z + 1, chips), chips, tell_beside, 0)

    both_sides(greet_side)

    for copy in other_load:
        copy.start()

    def count(*conditions):
        return sum(jnp.where(c, 1, 0) for c in conditions)

    sides = count(col > 0, col < columns - 1)
    pl.semaphore_wait(barrier, 1 + jnp.where(core == 1, 2 * z + 2 * jnp.minimum(z, LEADERS) * sides, count(z > 0)))

    def front_copy(to, n):
        cols = span(*spans[n])
        return pltpu.make_async_remote_copy(
            src_ref=front.at[:, :, cols], dst_ref=halo.at[:, :, cols],
            send_sem=halo_send, recv_sem=halo_recv.at[n],
            device_id=device(to, col), device_id_type=MESH,
        )

    @pl.when(slab > 0)
    def _():
        first_plane[0].wait()
        front_copy(slab - 1, 0).start()
        first_plane[1].wait()
        for n in range(1, len(spans)):
            front_copy(slab - 1, n).start()

    def told_ahead(chip, _):
        tell(behind, 2 * chip + core, col)
        return 0

    def aside(side, c):
        @pl.when(z > 0)
        def _():
            tell(behind, core, c)

    @pl.when(core == 1)
    def _():
        tell(told, other, col)

        @pl.when(z == 1)
        def _():
            tell(level, 0, col)
            tell(level, 1, col)

        lax.fori_loop(0, z, told_ahead, 0)
        both_sides(aside)

    @pl.when(slab == slabs - 1)
    def _():
        halo[...] = jnp.zeros_like(halo)

    @pl.when(core == 0)
    def _():
        pl.semaphore_wait(told, 1)
        lax.fori_loop(0, z, told_ahead, 0)
        both_sides(aside)

    def pair_copy(i):
        return pltpu.make_async_remote_copy(
            src_ref=pool.at[i, 2], dst_ref=pool.at[i, core],
            send_sem=pair_send, recv_sem=pair_recv.at[i],
            device_id=device(other, col), device_id_type=MESH,
        )

    def chip_copy(i):
        return pltpu.make_async_remote_copy(
            src_ref=packed.at[i], dst_ref=got.at[z],
            send_sem=chip_send, recv_sem=chip_recv.at[z],
            device_id=device(2 * i + core, col), device_id_type=MESH,
        )

    def border_copy(i, side, c):
        return pltpu.make_async_remote_copy(
            src_ref=border.at[i], dst_ref=border_got.at[1 - side, z],
            send_sem=border_send.at[side], recv_sem=border_recv.at[1 - side],
            device_id=device(2 * i + core, c), device_id_type=MESH,
        )

    left = lax.broadcasted_iota(jnp.int32, (8, LANES), 1) < LANES // 2
    left_slot = jnp.where(core == 0, 0, 2)
    right_slot = jnp.where(core == 0, 2, 1)

    def hear_front(n):
        @pl.when(slab < slabs - 1)
        def _():
            front_copy(slab, n).wait_recv()

    def march(i):
        parts = [
            march_group(field, halo, planes, fracs, counts, pl.ds(HALF * g, HALF), lanes(i), slab) for g in range(2)
        ]
        for n, (upper, lower) in enumerate(zip(*parts)):
            for m in range(2):
                up, down = upper[8 * m : 8 * m + 8], lower[8 * m : 8 * m + 8]
                pool[i, left_slot, n, pl.ds(8 * m, 8)] = jnp.where(left, up, pltpu.roll(down, LANES // 2, 1))
                pool[i, right_slot, n, pl.ds(8 * m, 8)] = jnp.where(left, pltpu.roll(up, LANES // 2, 1), down)
        pair_copy(i).start()

    def join(i):
        pair_copy(i).wait_recv()
        halves, edges = [], []
        for m in range(2):
            front = [pool[i, 0, n, pl.ds(8 * m, 8)] for n in range(5)]
            back = [pool[i, 1, n, pl.ds(8 * m, 8)] for n in range(5)]
            color = front[0] + front[2] * back[0]
            reach = front[1] + front[2] * back[1]
            coarse = front[3] + front[4] * back[3]
            fine, plain = front[2] * back[2], front[4] * back[4]
            halves.append([
                encode_log(color, COLOR_SPAN), encode_log(reach, DEPTH_SPAN), as_code(fine * TOP),
                encode_log(coarse, COLOR_SPAN), as_code(plain * TOP),
            ])
            edges.append([color, reach, fine, coarse, plain])
        for n, (first, last) in enumerate(zip(*edges)):
            border[i, pl.ds(n, 1)] = jnp.where(left[:1], first[:1], last[7:])
        words = [first | (last << 16) for first, last in zip(*halves)]

        @pl.when(i == z)
        def _():
            for n, word in enumerate(words):
                got[z, n] = word

        @pl.when(i != z)
        def _():
            for n, word in enumerate(words):
                packed[i, n] = word

    def send_border(i):
        both_sides(lambda side, c: border_copy(i, side, c).start())

    def finish(i):
        join(i)

        @pl.when(i < z)
        def _():
            chip_copy(i).start()

        @pl.when(i < jnp.minimum(z, LEADERS))
        def _():
            send_border(i)

    lag = jnp.where(z == chips - 1, 1, jnp.where(core == 0, AHEAD, 0))

    def step(i, _):
        @pl.when(i == 1)
        def _():
            for copy in other_load:
                copy.wait()
            hear_front(1)

        @pl.when(i == tiles // 2)
        def _():
            hear_front(2)

        @pl.when(i < tiles)
        def _():
            march(i)

        @pl.when(i >= lag)
        def _():
            finish(i - lag)

        return 0

    for copy in first_load:
        copy.wait()
    hear_front(0)
    lax.fori_loop(0, tiles + lag, step, 0)

    @pl.when(z < chips - 1)
    def _():
        pl.semaphore_wait(behind, (chips - 1 - z) * jnp.where(z == 0, 1 + sides, 1))

    @pl.when(z == 0)
    def _():
        def tell_level(chip, _):
            tell(level, 2 * chip + core, col)
            return 0

        lax.fori_loop(1, chips, tell_level, 0)

    def send_behind(i, _):
        chip_copy(i).start()
        return 0

    lax.fori_loop(z + 1, chips, send_behind, 0)

    pl.semaphore_wait(level, 1)

    def send_beside(i, _):
        send_border(i)
        return 0

    lax.fori_loop(jnp.minimum(z, LEADERS), chips, send_beside, 0)

    shape = (8, LANES)
    state = [[jnp.ones(shape, F32), jnp.ones(shape, F32)] + [jnp.zeros(shape, F32)] * 3 for _ in range(2)]
    for chip in range(chips):

        @pl.when(z != chip)
        def _():
            pltpu.make_async_remote_copy(
                src_ref=packed.at[0], dst_ref=got.at[chip], send_sem=chip_send, recv_sem=chip_recv.at[chip],
                device_id=device(slab, col), device_id_type=MESH,
            ).wait_recv()

        words = [got[chip, n] for n in range(5)]
        for half in range(2):
            codes = [(w & 0xFFFF) if half == 0 else (lax.shift_right_logical(w, 16)) for w in words]
            fine, plain, color, reach, coarse = state[half]
            color = color + fine * decode_log(codes[0], COLOR_SPAN)
            reach = reach + fine * decode_log(codes[1], DEPTH_SPAN)
            coarse = coarse + plain * decode_log(codes[3], COLOR_SPAN)
            fine = fine * (codes[2].astype(F32) * (1.0 / TOP))
            plain = plain * (codes[4].astype(F32) * (1.0 / TOP))
            state[half] = [fine, plain, color, reach, coarse]
    for half in range(2):
        fine, plain, color, reach, coarse = state[half]
        rows = pl.ds(8 * half, 8)
        image_out[0, rows] = color
        image_out[1, rows] = (reach - SHIFT * (1.0 - fine)) * (1.0 / 2048)
        image_out[2, rows] = coarse

    def all_borders(side, c):
        return pltpu.make_async_remote_copy(
            src_ref=border, dst_ref=border_got.at[side], send_sem=border_send.at[side], recv_sem=border_recv.at[side],
            device_id=device(slab, c), device_id_type=MESH,
        )

    both_sides(lambda side, c: all_borders(side, c).wait_recv())
    line = (1, LANES)
    fine, plain = jnp.ones(line, F32), jnp.ones(line, F32)
    color, reach, coarse = [jnp.zeros(line, F32)] * 3
    for chip in range(chips):
        parts = [
            jnp.where(left[:1], border_got[1, chip, pl.ds(n, 1)], border_got[0, chip, pl.ds(n, 1)]) for n in range(5)
        ]
        color, reach, coarse = color + fine * parts[0], reach + fine * parts[1], coarse + plain * parts[3]
        fine, plain = fine * parts[2], plain * parts[4]
    there = jnp.where(left, jnp.where(col < columns - 1, 1.0, 0.0), jnp.where(col > 0, 1.0, 0.0))
    for n, row in enumerate((color, (reach - SHIFT * (1.0 - fine)) * (1.0 / 2048), coarse)):
        row = jnp.where(there > 0.5, jnp.broadcast_to(row, (8, LANES)), 0.0)
        image_out[n, pl.ds(2 * 8, 8)] = pltpu.roll(row, LANES // 2, 1)

    @pl.when(slab > 0)
    def _():
        pltpu.make_async_remote_copy(
            src_ref=front, dst_ref=halo, send_sem=halo_send, recv_sem=halo_recv.at[0],
            device_id=device(slab - 1, col), device_id_type=MESH,
        ).wait_send()

    pltpu.make_async_remote_copy(
        src_ref=pool.at[:, 2], dst_ref=pool.at[:, core], send_sem=pair_send, recv_sem=pair_recv.at[0],
        device_id=device(other, col), device_id_type=MESH,
    ).wait_send()
    others = pl.ds(0, tiles - 1)
    pltpu.make_async_remote_copy(
        src_ref=packed.at[others], dst_ref=got.at[others], send_sem=chip_send, recv_sem=chip_recv.at[0],
        device_id=device(other, col), device_id_type=MESH,
    ).wait_send()
    both_sides(lambda side, c: all_borders(side, c).wait_send())


def smooth_kernel(image, color_out, depth_out, coarse_out, padded):
    half = LANES // 2
    for n, out in enumerate((color_out, depth_out, coarse_out)):
        whole = image[n]
        turned = pltpu.roll(whole, half, 1)
        padded[n, pl.ds(7, 1)] = whole[16:17]
        padded[n, pl.ds(8, HALF)] = whole[:HALF]
        padded[n, pl.ds(8 + HALF, HALF)] = turned[:HALF]
        padded[n, pl.ds(8 + 2 * HALF, 1)] = turned[16:17]
        smooth = 0.25 * padded[n, pl.ds(7, 32)] + 0.5 * padded[n, pl.ds(8, 32)] + 0.25 * padded[n, pl.ds(9, 32)]
        out[...] = smooth[:, :half]


def body(field, fine_plane, fine_frac, counts):
    channels, depth, rows, width = field.shape
    slots = fine_plane.shape[0]
    tiles = width // LANES
    dma = pltpu.SemaphoreType.DMA
    out = jax.ShapeDtypeStruct((rows, LANES // 2), F32)
    vmem = pl.BlockSpec(memory_space=pltpu.VMEM)
    anywhere = pl.BlockSpec(memory_space=pltpu.HBM)
    image = pl.pallas_call(
        kernel,
        out_shape=jax.ShapeDtypeStruct((3, 24, LANES), F32),
        in_specs=[anywhere] * 4,
        out_specs=vmem,
        scratch_shapes=[
            pltpu.VMEM((channels, depth, rows, width), jnp.bfloat16),
            pltpu.VMEM((channels, rows, width), jnp.bfloat16),
            pltpu.VMEM((channels, rows, width), jnp.bfloat16),
            pltpu.VMEM((slots, rows, width), jnp.int32),
            pltpu.VMEM((slots, rows, width), jnp.int32),
            pltpu.VMEM((1, rows, width), jnp.int32),
            pltpu.VMEM((tiles, 3, 5, HALF, LANES), F32),
            pltpu.VMEM((tiles, 5, 8, LANES), jnp.int32),
            pltpu.VMEM((tiles, 5, 8, LANES), jnp.int32),
            pltpu.VMEM((tiles, 8, LANES), F32),
            pltpu.VMEM((2, tiles, 8, LANES), F32),
            dma((5, 2)),
            dma, dma((3,)),
            dma, dma((tiles,)),
            dma, dma((tiles,)),
            dma((2,)), dma((2,)),
            pltpu.SemaphoreType.REGULAR, pltpu.SemaphoreType.REGULAR, pltpu.SemaphoreType.REGULAR,
        ],
        compiler_params=pltpu.CompilerParams(collective_id=0, has_side_effects=True, vmem_limit_bytes=56400000),
        name="render",
    )(field, fine_plane, fine_frac, counts)
    return pl.pallas_call(
        smooth_kernel,
        out_shape=(out, out, out),
        in_specs=[vmem],
        out_specs=(vmem, vmem, vmem),
        scratch_shapes=[pltpu.VMEM((3, rows + 16, LANES), F32)],
        compiler_params=pltpu.CompilerParams(vmem_limit_bytes=4 << 20),
        name="smooth",
    )(image)


def solution(mesh):
    in_specs = (
        P(None, "slab", "col", None),
        P("slab", "col", None),
        P("slab", "col", None),
        P("slab", "col", None),
    )
    out_specs = (P("col", "slab"), P("col", "slab"), P("col", "slab"))
    return jax.shard_map(body, mesh=mesh, in_specs=in_specs, out_specs=out_specs, check_vma=False)
```

```python
import jax
import jax.numpy as jnp
from jax import lax
from jax.experimental import pallas as pl
from jax.experimental.pallas import tpu as pltpu
from jax.sharding import PartitionSpec as P

F32 = jnp.float32
MESH = pl.DeviceIdType.MESH
LANES = 128
AHEAD = 4
LEADERS = 3
HALF = 16
LOG2E = 1.4426950408889634
SHIFT = 0.5
TOP = 65535.0
COLOR_SPAN = (-22.5, 0.0)
DEPTH_SPAN = (-15.0, 10.75)


def pick(leaves, masks):
    for mask in masks:
        pairs = [jnp.where(mask, leaves[i + 1], leaves[i]) for i in range(0, len(leaves) - 1, 2)]
        leaves = pairs + leaves[2 * len(pairs) :]
    return leaves[0]


def softplus2(values):
    return jnp.log2(1.0 + jnp.exp2(values * LOG2E))


def march_group(field, halo, planes, fracs, counts, rows, cols, slab):
    depth = field.shape[1]
    slots = planes.shape[0]
    total = depth * 16
    scale = 2.0 / total

    def leaf(channel, plane):
        if plane == depth:
            return halo[channel, rows, cols]
        return field[channel, plane, rows, cols]

    shape = (HALF, LANES)
    live = counts[0, rows, cols]
    through, color, reach = jnp.ones(shape, F32), jnp.zeros(shape, F32), jnp.zeros(shape, F32)
    first = (slab * depth * 8).astype(F32) + SHIFT
    i16 = jnp.int16
    for slot in range(slots):
        plane = planes[slot, rows, cols]
        spot = (plane << 3) + fracs[slot, rows, cols]
        p = plane.astype(i16)
        up = p + i16(1)
        odd_bits = [(p & i16(2)) != i16(0), (p & i16(4)) != i16(0), p >= i16(8)]
        even_bits = [(up & i16(2)) != i16(0), (up & i16(4)) != i16(0), up >= i16(8), up >= i16(16)]
        even_weight = jnp.abs((spot & 15).astype(F32) * 0.125 - 1.0)
        values = []
        for channel in range(2):
            odd = pick([leaf(channel, k) for k in range(1, depth, 2)], odd_bits).astype(F32)
            even = pick([leaf(channel, k) for k in range(0, depth + 1, 2)], even_bits).astype(F32)
            values.append(odd + (even - odd) * even_weight)
        factor = jnp.exp2(softplus2(values[0]) * (-scale * depth / slots))
        after = through * jnp.where(live > slot, factor, 1.0)
        weight = through - after
        through = after
        color = color + weight * (1.0 + jnp.tanh(0.5 * values[1]))
        reach = reach + weight * (spot.astype(F32) + first)
    coarse_through, coarse = jnp.ones(shape, F32), jnp.zeros(shape, F32)
    for k in range(7, depth, 8):
        value, shine = [
            0.5 * (leaf(channel, k).astype(F32) + leaf(channel, k + 1).astype(F32)) for channel in range(2)
        ]
        after = coarse_through * jnp.exp2(softplus2(value) * (-8.0 * scale))
        coarse = coarse + (coarse_through - after) * (1.0 + jnp.tanh(0.5 * shine))
        coarse_through = after
    return 0.5 * color, reach, through, 0.5 * coarse, coarse_through


def as_code(u):
    return (jnp.clip(u, 0.0, TOP) + 0.5).astype(jnp.int32)


def encode_log(values, span):
    low, high = span
    step = TOP / (high - low)
    return as_code(jnp.log2(values) * step - low * step)


def decode_log(code, span):
    low, high = span
    return jnp.exp2(code.astype(F32) * ((high - low) / TOP) + low)


def kernel(
    field_in, plane_in, frac_in, count_in,
    image_out,
    field, front, halo, planes, fracs, counts, pool, packed, got, border, border_got,
    load_sem, halo_send, halo_recv, pair_send, pair_recv, chip_send, chip_recv, border_send, border_recv, behind, level, told,
):
    slab, col = lax.axis_index("slab"), lax.axis_index("col")
    slabs, columns = lax.axis_size("slab"), lax.axis_size("col")
    chips = slabs // 2
    z, core = slab // 2, slab % 2
    other = slab + 1 - 2 * core
    tiles = chips

    def device(s, c):
        return {"slab": s, "col": c}

    def lanes(tile):
        return pl.ds(pl.multiple_of(tile * LANES, LANES), LANES)

    spans = [(0, 1), (1, tiles // 2), (tiles // 2, tiles)]

    def span(first, last):
        return pl.ds(first * LANES, (last - first) * LANES)

    def loads(n, cols):
        return [
            pltpu.make_async_copy(field_in.at[:, :, :, cols], field.at[:, :, :, cols], load_sem.at[0, n]),
            pltpu.make_async_copy(plane_in.at[:, :, cols], planes.at[:, :, cols], load_sem.at[1, n]),
            pltpu.make_async_copy(frac_in.at[:, :, cols], fracs.at[:, :, cols], load_sem.at[2, n]),
            pltpu.make_async_copy(count_in.at[:, :, cols], counts.at[:, :, cols], load_sem.at[3, n]),
        ]

    first_load, other_load = loads(0, span(0, 1)), loads(1, span(1, tiles))

    barrier = pltpu.get_barrier_semaphore()

    def tell(semaphore, s, c):
        pl.semaphore_signal(semaphore, inc=1, device_id=device(s, c), device_id_type=MESH)

    first_plane = [
        pltpu.make_async_copy(field_in.at[:, 0, :, cols], front.at[:, :, cols], load_sem.at[4, n])
        for n, cols in enumerate((span(0, 1), span(1, tiles)))
    ]

    @pl.when(slab > 0)
    def _():
        for copy in first_plane:
            copy.start()

    tell(barrier, other, col)

    @pl.when(jnp.logical_and(core == 1, z < chips - 1))
    def _():
        tell(barrier, slab + 1, col)

    for copy in first_load:
        copy.start()

    def tell_behind(chip, _):
        tell(barrier, 2 * chip + 1, col)
        return 0

    lax.fori_loop(z + 1, chips, tell_behind, 0)

    def both_sides(act):
        @pl.when(col > 0)
        def _():
            act(0, col - 1)

        @pl.when(col < columns - 1)
        def _():
            act(1, col + 1)

    def greet_side(side, c):
        def tell_beside(chip, _):
            tell(barrier, 2 * chip + 1, c)
            return 0

        lax.fori_loop(jnp.where(z < LEADERS, z + 1, chips), chips, tell_beside, 0)

    both_sides(greet_side)

    for copy in other_load:
        copy.start()

    def count(*conditions):
        return sum(jnp.where(c, 1, 0) for c in conditions)

    sides = count(col > 0, col < columns - 1)
    pl.semaphore_wait(barrier, 1 + jnp.where(core == 1, 2 * z + 2 * jnp.minimum(z, LEADERS) * sides, count(z > 0)))

    def front_copy(to, n):
        cols = span(*spans[n])
        return pltpu.make_async_remote_copy(
            src_ref=front.at[:, :, cols], dst_ref=halo.at[:, :, cols],
            send_sem=halo_send, recv_sem=halo_recv.at[n],
            device_id=device(to, col), device_id_type=MESH,
        )

    @pl.when(slab > 0)
    def _():
        first_plane[0].wait()
        front_copy(slab - 1, 0).start()
        first_plane[1].wait()
        for n in range(1, len(spans)):
            front_copy(slab - 1, n).start()

    def told_ahead(chip, _):
        tell(behind, 2 * chip + core, col)
        return 0

    def aside(side, c):
        @pl.when(z > 0)
        def _():
            tell(behind, core, c)

    @pl.when(core == 1)
    def _():
        tell(told, other, col)

        @pl.when(z == 1)
        def _():
            tell(level, 0, col)
            tell(level, 1, col)

        lax.fori_loop(0, z, told_ahead, 0)
        both_sides(aside)

    @pl.when(slab == slabs - 1)
    def _():
        halo[...] = jnp.zeros_like(halo)

    @pl.when(core == 0)
    def _():
        pl.semaphore_wait(told, 1)
        lax.fori_loop(0, z, told_ahead, 0)
        both_sides(aside)

    def pair_copy(i):
        return pltpu.make_async_remote_copy(
            src_ref=pool.at[i, 2], dst_ref=pool.at[i, core],
            send_sem=pair_send, recv_sem=pair_recv.at[i],
            device_id=device(other, col), device_id_type=MESH,
        )

    def chip_copy(i):
        return pltpu.make_async_remote_copy(
            src_ref=packed.at[i], dst_ref=got.at[z],
            send_sem=chip_send, recv_sem=chip_recv.at[z],
            device_id=device(2 * i + core, col), device_id_type=MESH,
        )

    def border_copy(i, side, c):
        return pltpu.make_async_remote_copy(
            src_ref=border.at[i], dst_ref=border_got.at[1 - side, z],
            send_sem=border_send.at[side], recv_sem=border_recv.at[1 - side],
            device_id=device(2 * i + core, c), device_id_type=MESH,
        )

    left = lax.broadcasted_iota(jnp.int32, (8, LANES), 1) < LANES // 2
    left_slot = jnp.where(core == 0, 0, 2)
    right_slot = jnp.where(core == 0, 2, 1)

    def hear_front(n):
        @pl.when(slab < slabs - 1)
        def _():
            front_copy(slab, n).wait_recv()

    def march(i):
        parts = [
            march_group(field, halo, planes, fracs, counts, pl.ds(HALF * g, HALF), lanes(i), slab) for g in range(2)
        ]
        for n, (upper, lower) in enumerate(zip(*parts)):
            for m in range(2):
                up, down = upper[8 * m : 8 * m + 8], lower[8 * m : 8 * m + 8]
                pool[i, left_slot, n, pl.ds(8 * m, 8)] = jnp.where(left, up, pltpu.roll(down, LANES // 2, 1))
                pool[i, right_slot, n, pl.ds(8 * m, 8)] = jnp.where(left, pltpu.roll(up, LANES // 2, 1), down)
        pair_copy(i).start()

    def join(i):
        pair_copy(i).wait_recv()
        halves, edges = [], []
        for m in range(2):
            front = [pool[i, 0, n, pl.ds(8 * m, 8)] for n in range(5)]
            back = [pool[i, 1, n, pl.ds(8 * m, 8)] for n in range(5)]
            color = front[0] + front[2] * back[0]
            reach = front[1] + front[2] * back[1]
            coarse = front[3] + front[4] * back[3]
            fine, plain = front[2] * back[2], front[4] * back[4]
            halves.append([
                encode_log(color, COLOR_SPAN), encode_log(reach, DEPTH_SPAN), as_code(fine * TOP),
                encode_log(coarse, COLOR_SPAN), as_code(plain * TOP),
            ])
            edges.append([color, reach, fine, coarse, plain])
        for n, (first, last) in enumerate(zip(*edges)):
            border[i, pl.ds(n, 1)] = jnp.where(left[:1], first[:1], last[7:])
        words = [first | (last << 16) for first, last in zip(*halves)]

        @pl.when(i == z)
        def _():
            for n, word in enumerate(words):
                got[z, n] = word

        @pl.when(i != z)
        def _():
            for n, word in enumerate(words):
                packed[i, n] = word

    def send_border(i):
        both_sides(lambda side, c: border_copy(i, side, c).start())

    def finish(i):
        join(i)

        @pl.when(i < z)
        def _():
            chip_copy(i).start()

        @pl.when(jnp.logical_and(z > LEADERS, i == LEADERS))
        def _():
            pl.semaphore_wait(level, 1)

        @pl.when(jnp.logical_or(z > LEADERS, i < z))
        def _():
            @pl.when(jnp.logical_or(z > LEADERS, i < LEADERS))
            def _():
                send_border(i)

    lag = jnp.where(z == chips - 1, 1, jnp.where(core == 0, AHEAD, 0))

    def step(i, _):
        @pl.when(i == 1)
        def _():
            for copy in other_load:
                copy.wait()
            hear_front(1)

        @pl.when(i == tiles // 2)
        def _():
            hear_front(2)

        @pl.when(i < tiles)
        def _():
            march(i)

        @pl.when(i >= lag)
        def _():
            finish(i - lag)

        return 0

    for copy in first_load:
        copy.wait()
    hear_front(0)
    lax.fori_loop(0, tiles + lag, step, 0)

    @pl.when(z < chips - 1)
    def _():
        pl.semaphore_wait(behind, (chips - 1 - z) * jnp.where(z == 0, 1 + sides, 1))

    @pl.when(z == 0)
    def _():
        def tell_level(chip, _):
            tell(level, 2 * chip + core, col)
            return 0

        lax.fori_loop(1, chips, tell_level, 0)

    def send_behind(i, _):
        chip_copy(i).start()
        return 0

    lax.fori_loop(z + 1, chips, send_behind, 0)

    @pl.when(z <= LEADERS)
    def _():
        pl.semaphore_wait(level, 1)

        def send_beside(i, _):
            send_border(i)
            return 0

        lax.fori_loop(z, chips, send_beside, 0)

    shape = (8, LANES)
    state = [[jnp.ones(shape, F32), jnp.ones(shape, F32)] + [jnp.zeros(shape, F32)] * 3 for _ in range(2)]
    for chip in range(chips):

        @pl.when(z != chip)
        def _():
            pltpu.make_async_remote_copy(
                src_ref=packed.at[0], dst_ref=got.at[chip], send_sem=chip_send, recv_sem=chip_recv.at[chip],
                device_id=device(slab, col), device_id_type=MESH,
            ).wait_recv()

        words = [got[chip, n] for n in range(5)]
        for half in range(2):
            codes = [(w & 0xFFFF) if half == 0 else (lax.shift_right_logical(w, 16)) for w in words]
            fine, plain, color, reach, coarse = state[half]
            color = color + fine * decode_log(codes[0], COLOR_SPAN)
            reach = reach + fine * decode_log(codes[1], DEPTH_SPAN)
            coarse = coarse + plain * decode_log(codes[3], COLOR_SPAN)
            fine = fine * (codes[2].astype(F32) * (1.0 / TOP))
            plain = plain * (codes[4].astype(F32) * (1.0 / TOP))
            state[half] = [fine, plain, color, reach, coarse]
    for half in range(2):
        fine, plain, color, reach, coarse = state[half]
        rows = pl.ds(8 * half, 8)
        image_out[0, rows] = color
        image_out[1, rows] = (reach - SHIFT * (1.0 - fine)) * (1.0 / 2048)
        image_out[2, rows] = coarse

    def all_borders(side, c):
        return pltpu.make_async_remote_copy(
            src_ref=border, dst_ref=border_got.at[side], send_sem=border_send.at[side], recv_sem=border_recv.at[side],
            device_id=device(slab, c), device_id_type=MESH,
        )

    both_sides(lambda side, c: all_borders(side, c).wait_recv())
    line = (1, LANES)
    fine, plain = jnp.ones(line, F32), jnp.ones(line, F32)
    color, reach, coarse = [jnp.zeros(line, F32)] * 3
    for chip in range(chips):
        parts = [
            jnp.where(left[:1], border_got[1, chip, pl.ds(n, 1)], border_got[0, chip, pl.ds(n, 1)]) for n in range(5)
        ]
        color, reach, coarse = color + fine * parts[0], reach + fine * parts[1], coarse + plain * parts[3]
        fine, plain = fine * parts[2], plain * parts[4]
    there = jnp.where(left, jnp.where(col < columns - 1, 1.0, 0.0), jnp.where(col > 0, 1.0, 0.0))
    for n, row in enumerate((color, (reach - SHIFT * (1.0 - fine)) * (1.0 / 2048), coarse)):
        row = jnp.where(there > 0.5, jnp.broadcast_to(row, (8, LANES)), 0.0)
        image_out[n, pl.ds(2 * 8, 8)] = pltpu.roll(row, LANES // 2, 1)

    @pl.when(slab > 0)
    def _():
        pltpu.make_async_remote_copy(
            src_ref=front, dst_ref=halo, send_sem=halo_send, recv_sem=halo_recv.at[0],
            device_id=device(slab - 1, col), device_id_type=MESH,
        ).wait_send()

    pltpu.make_async_remote_copy(
        src_ref=pool.at[:, 2], dst_ref=pool.at[:, core], send_sem=pair_send, recv_sem=pair_recv.at[0],
        device_id=device(other, col), device_id_type=MESH,
    ).wait_send()
    others = pl.ds(0, tiles - 1)
    pltpu.make_async_remote_copy(
        src_ref=packed.at[others], dst_ref=got.at[others], send_sem=chip_send, recv_sem=chip_recv.at[0],
        device_id=device(other, col), device_id_type=MESH,
    ).wait_send()
    both_sides(lambda side, c: all_borders(side, c).wait_send())


def smooth_kernel(image, color_out, depth_out, coarse_out, padded):
    half = LANES // 2
    for n, out in enumerate((color_out, depth_out, coarse_out)):
        whole = image[n]
        turned = pltpu.roll(whole, half, 1)
        padded[n, pl.ds(7, 1)] = whole[16:17]
        padded[n, pl.ds(8, HALF)] = whole[:HALF]
        padded[n, pl.ds(8 + HALF, HALF)] = turned[:HALF]
        padded[n, pl.ds(8 + 2 * HALF, 1)] = turned[16:17]
        smooth = 0.25 * padded[n, pl.ds(7, 32)] + 0.5 * padded[n, pl.ds(8, 32)] + 0.25 * padded[n, pl.ds(9, 32)]
        out[...] = smooth[:, :half]


def body(field, fine_plane, fine_frac, counts):
    channels, depth, rows, width = field.shape
    slots = fine_plane.shape[0]
    tiles = width // LANES
    dma = pltpu.SemaphoreType.DMA
    out = jax.ShapeDtypeStruct((rows, LANES // 2), F32)
    vmem = pl.BlockSpec(memory_space=pltpu.VMEM)
    anywhere = pl.BlockSpec(memory_space=pltpu.HBM)
    image = pl.pallas_call(
        kernel,
        out_shape=jax.ShapeDtypeStruct((3, 24, LANES), F32),
        in_specs=[anywhere] * 4,
        out_specs=vmem,
        scratch_shapes=[
            pltpu.VMEM((channels, depth, rows, width), jnp.bfloat16),
            pltpu.VMEM((channels, rows, width), jnp.bfloat16),
            pltpu.VMEM((channels, rows, width), jnp.bfloat16),
            pltpu.VMEM((slots, rows, width), jnp.int32),
            pltpu.VMEM((slots, rows, width), jnp.int32),
            pltpu.VMEM((1, rows, width), jnp.int32),
            pltpu.VMEM((tiles, 3, 5, HALF, LANES), F32),
            pltpu.VMEM((tiles, 5, 8, LANES), jnp.int32),
            pltpu.VMEM((tiles, 5, 8, LANES), jnp.int32),
            pltpu.VMEM((tiles, 8, LANES), F32),
            pltpu.VMEM((2, tiles, 8, LANES), F32),
            dma((5, 2)),
            dma, dma((3,)),
            dma, dma((tiles,)),
            dma, dma((tiles,)),
            dma((2,)), dma((2,)),
            pltpu.SemaphoreType.REGULAR, pltpu.SemaphoreType.REGULAR, pltpu.SemaphoreType.REGULAR,
        ],
        compiler_params=pltpu.CompilerParams(collective_id=0, has_side_effects=True, vmem_limit_bytes=56400000),
        name="render",
    )(field, fine_plane, fine_frac, counts)
    return pl.pallas_call(
        smooth_kernel,
        out_shape=(out, out, out),
        in_specs=[vmem],
        out_specs=(vmem, vmem, vmem),
        scratch_shapes=[pltpu.VMEM((3, rows + 16, LANES), F32)],
        compiler_params=pltpu.CompilerParams(vmem_limit_bytes=4 << 20),
        name="smooth",
    )(image)


def solution(mesh):
    in_specs = (
        P(None, "slab", "col", None),
        P("slab", "col", None),
        P("slab", "col", None),
        P("slab", "col", None),
    )
    out_specs = (P("col", "slab"), P("col", "slab"), P("col", "slab"))
    return jax.shard_map(body, mesh=mesh, in_specs=in_specs, out_specs=out_specs, check_vma=False)
```

```python
import jax
import jax.numpy as jnp
from jax import lax
from jax.experimental import pallas as pl
from jax.experimental.pallas import tpu as pltpu
from jax.sharding import PartitionSpec as P

F32 = jnp.float32
MESH = pl.DeviceIdType.MESH
LANES = 128
AHEAD = 4
LEADERS = 3
HALF = 16
LOG2E = 1.4426950408889634
SHIFT = 0.5
TOP = 65535.0
COLOR_SPAN = (-22.5, 0.0)
DEPTH_SPAN = (-15.0, 10.75)


def pick(leaves, masks):
    for mask in masks:
        pairs = [jnp.where(mask, leaves[i + 1], leaves[i]) for i in range(0, len(leaves) - 1, 2)]
        leaves = pairs + leaves[2 * len(pairs) :]
    return leaves[0]


def softplus2(values):
    return jnp.log2(1.0 + jnp.exp2(values * LOG2E))


def march_group(field, halo, planes, fracs, counts, rows, cols, slab):
    depth = field.shape[1]
    slots = planes.shape[0]
    total = depth * 16
    scale = 2.0 / total

    def leaf(channel, plane):
        if plane == depth:
            return halo[channel, rows, cols]
        return field[channel, plane, rows, cols]

    shape = (HALF, LANES)
    live = counts[0, rows, cols]
    through, color, reach = jnp.ones(shape, F32), jnp.zeros(shape, F32), jnp.zeros(shape, F32)
    first = (slab * depth * 8).astype(F32) + SHIFT
    i16 = jnp.int16
    for slot in range(slots):
        plane = planes[slot, rows, cols]
        spot = (plane << 3) + fracs[slot, rows, cols]
        p = plane.astype(i16)
        up = p + i16(1)
        odd_bits = [(p & i16(2)) != i16(0), (p & i16(4)) != i16(0), p >= i16(8)]
        even_bits = [(up & i16(2)) != i16(0), (up & i16(4)) != i16(0), up >= i16(8), up >= i16(16)]
        even_weight = jnp.abs((spot & 15).astype(F32) * 0.125 - 1.0)
        values = []
        for channel in range(2):
            odd = pick([leaf(channel, k) for k in range(1, depth, 2)], odd_bits).astype(F32)
            even = pick([leaf(channel, k) for k in range(0, depth + 1, 2)], even_bits).astype(F32)
            values.append(odd + (even - odd) * even_weight)
        factor = jnp.exp2(softplus2(values[0]) * (-scale * depth / slots))
        after = through * jnp.where(live > slot, factor, 1.0)
        weight = through - after
        through = after
        color = color + weight * (1.0 + jnp.tanh(0.5 * values[1]))
        reach = reach + weight * (spot.astype(F32) + first)
    coarse_through, coarse = jnp.ones(shape, F32), jnp.zeros(shape, F32)
    for k in range(7, depth, 8):
        value, shine = [
            0.5 * (leaf(channel, k).astype(F32) + leaf(channel, k + 1).astype(F32)) for channel in range(2)
        ]
        after = coarse_through * jnp.exp2(softplus2(value) * (-8.0 * scale))
        coarse = coarse + (coarse_through - after) * (1.0 + jnp.tanh(0.5 * shine))
        coarse_through = after
    return 0.5 * color, reach, through, 0.5 * coarse, coarse_through


def as_code(u):
    return (jnp.clip(u, 0.0, TOP) + 0.5).astype(jnp.int32)


def encode_log(values, span):
    low, high = span
    step = TOP / (high - low)
    return as_code(jnp.log2(values) * step - low * step)


def decode_log(code, span):
    low, high = span
    return jnp.exp2(code.astype(F32) * ((high - low) / TOP) + low)


def kernel(
    field_in, plane_in, frac_in, count_in,
    image_out,
    field, front, halo, planes, fracs, counts, pool, packed, got, border, border_got,
    load_sem, halo_send, halo_recv, pair_send, pair_recv, chip_send, chip_recv, border_send, border_recv, behind, level, told,
):
    slab, col = lax.axis_index("slab"), lax.axis_index("col")
    slabs, columns = lax.axis_size("slab"), lax.axis_size("col")
    chips = slabs // 2
    z, core = slab // 2, slab % 2
    other = slab + 1 - 2 * core
    tiles = chips

    def device(s, c):
        return {"slab": s, "col": c}

    def lanes(tile):
        return pl.ds(pl.multiple_of(tile * LANES, LANES), LANES)

    spans = [(0, 1), (1, tiles // 2), (tiles // 2, tiles)]

    def span(first, last):
        return pl.ds(first * LANES, (last - first) * LANES)

    def loads(n, cols):
        return [
            pltpu.make_async_copy(field_in.at[:, :, :, cols], field.at[:, :, :, cols], load_sem.at[0, n]),
            pltpu.make_async_copy(plane_in.at[:, :, cols], planes.at[:, :, cols], load_sem.at[1, n]),
            pltpu.make_async_copy(frac_in.at[:, :, cols], fracs.at[:, :, cols], load_sem.at[2, n]),
            pltpu.make_async_copy(count_in.at[:, :, cols], counts.at[:, :, cols], load_sem.at[3, n]),
        ]

    first_load, other_load = loads(0, span(0, 1)), loads(1, span(1, tiles))

    barrier = pltpu.get_barrier_semaphore()

    def tell(semaphore, s, c):
        pl.semaphore_signal(semaphore, inc=1, device_id=device(s, c), device_id_type=MESH)

    first_plane = [
        pltpu.make_async_copy(field_in.at[:, 0, :, cols], front.at[:, :, cols], load_sem.at[4, n])
        for n, cols in enumerate((span(0, 1), span(1, tiles)))
    ]

    @pl.when(slab > 0)
    def _():
        for copy in first_plane:
            copy.start()

    tell(barrier, other, col)

    @pl.when(jnp.logical_and(core == 1, z < chips - 1))
    def _():
        tell(barrier, slab + 1, col)

    for copy in first_load:
        copy.start()

    def tell_behind(chip, _):
        tell(barrier, 2 * chip + 1, col)
        return 0

    lax.fori_loop(z + 1, chips, tell_behind, 0)

    def both_sides(act):
        @pl.when(col > 0)
        def _():
            act(0, col - 1)

        @pl.when(col < columns - 1)
        def _():
            act(1, col + 1)

    def greet_side(side, c):
        def tell_beside(chip, _):
            tell(barrier, 2 * chip + 1, c)
            return 0

        lax.fori_loop(jnp.where(z < LEADERS, z + 1, chips), chips, tell_beside, 0)

    both_sides(greet_side)

    for copy in other_load:
        copy.start()

    def count(*conditions):
        return sum(jnp.where(c, 1, 0) for c in conditions)

    sides = count(col > 0, col < columns - 1)
    pl.semaphore_wait(barrier, 1 + jnp.where(core == 1, 2 * z + 2 * jnp.minimum(z, LEADERS) * sides, count(z > 0)))

    def front_copy(to, n):
        cols = span(*spans[n])
        return pltpu.make_async_remote_copy(
            src_ref=front.at[:, :, cols], dst_ref=halo.at[:, :, cols],
            send_sem=halo_send, recv_sem=halo_recv.at[n],
            device_id=device(to, col), device_id_type=MESH,
        )

    @pl.when(slab > 0)
    def _():
        first_plane[0].wait()
        front_copy(slab - 1, 0).start()
        first_plane[1].wait()
        for n in range(1, len(spans)):
            front_copy(slab - 1, n).start()

    def told_ahead(chip, _):
        tell(behind, 2 * chip + core, col)
        return 0

    def aside(side, c):
        @pl.when(z > 0)
        def _():
            tell(behind, core, c)

    @pl.when(core == 1)
    def _():
        tell(told, other, col)

        @pl.when(z == 1)
        def _():
            tell(level, 0, col)
            tell(level, 1, col)

        lax.fori_loop(0, z, told_ahead, 0)
        both_sides(aside)

    @pl.when(slab == slabs - 1)
    def _():
        halo[...] = jnp.zeros_like(halo)

    @pl.when(core == 0)
    def _():
        pl.semaphore_wait(told, 1)
        lax.fori_loop(0, z, told_ahead, 0)
        both_sides(aside)

    def pair_copy(i):
        return pltpu.make_async_remote_copy(
            src_ref=pool.at[i, 2], dst_ref=pool.at[i, core],
            send_sem=pair_send, recv_sem=pair_recv.at[i],
            device_id=device(other, col), device_id_type=MESH,
        )

    def chip_copy(i):
        return pltpu.make_async_remote_copy(
            src_ref=packed.at[i], dst_ref=got.at[z],
            send_sem=chip_send, recv_sem=chip_recv.at[z],
            device_id=device(2 * i + core, col), device_id_type=MESH,
        )

    def border_copy(i, side, c):
        return pltpu.make_async_remote_copy(
            src_ref=border.at[i], dst_ref=border_got.at[1 - side, z],
            send_sem=border_send.at[side], recv_sem=border_recv.at[1 - side],
            device_id=device(2 * i + core, c), device_id_type=MESH,
        )

    left = lax.broadcasted_iota(jnp.int32, (8, LANES), 1) < LANES // 2
    left_slot = jnp.where(core == 0, 0, 2)
    right_slot = jnp.where(core == 0, 2, 1)

    def hear_front(n):
        @pl.when(slab < slabs - 1)
        def _():
            front_copy(slab, n).wait_recv()

    def march(i):
        parts = [
            march_group(field, halo, planes, fracs, counts, pl.ds(HALF * g, HALF), lanes(i), slab) for g in range(2)
        ]
        for n, (upper, lower) in enumerate(zip(*parts)):
            for m in range(2):
                up, down = upper[8 * m : 8 * m + 8], lower[8 * m : 8 * m + 8]
                pool[i, left_slot, n, pl.ds(8 * m, 8)] = jnp.where(left, up, pltpu.roll(down, LANES // 2, 1))
                pool[i, right_slot, n, pl.ds(8 * m, 8)] = jnp.where(left, pltpu.roll(up, LANES // 2, 1), down)
        pair_copy(i).start()

    def join(i):
        pair_copy(i).wait_recv()
        halves, edges = [], []
        for m in range(2):
            front = [pool[i, 0, n, pl.ds(8 * m, 8)] for n in range(5)]
            back = [pool[i, 1, n, pl.ds(8 * m, 8)] for n in range(5)]
            color = front[0] + front[2] * back[0]
            reach = front[1] + front[2] * back[1]
            coarse = front[3] + front[4] * back[3]
            fine, plain = front[2] * back[2], front[4] * back[4]
            halves.append([
                encode_log(color, COLOR_SPAN), encode_log(reach, DEPTH_SPAN), as_code(fine * TOP),
                encode_log(coarse, COLOR_SPAN), as_code(plain * TOP),
            ])
            edges.append([color, reach, fine, coarse, plain])
        for n, (first, last) in enumerate(zip(*edges)):
            border[i, pl.ds(n, 1)] = jnp.where(left[:1], first[:1], last[7:])
        words = [first | (last << 16) for first, last in zip(*halves)]

        @pl.when(i == z)
        def _():
            for n, word in enumerate(words):
                got[z, n] = word

        @pl.when(i != z)
        def _():
            for n, word in enumerate(words):
                packed[i, n] = word

    def send_border(i):
        both_sides(lambda side, c: border_copy(i, side, c).start())

    def finish(i):
        join(i)

        @pl.when(jnp.logical_and(z > LEADERS, i == LEADERS))
        def _():
            pl.semaphore_wait(level, 1)

        @pl.when(jnp.logical_or(z > LEADERS, i < z))
        def _():
            @pl.when(jnp.logical_or(z > LEADERS, i < LEADERS))
            def _():
                send_border(i)

        @pl.when(i < z)
        def _():
            chip_copy(i).start()

    lag = jnp.where(z == chips - 1, 1, jnp.where(core == 0, AHEAD, 0))

    def step(i, _):
        @pl.when(i == 1)
        def _():
            for copy in other_load:
                copy.wait()
            hear_front(1)

        @pl.when(i == tiles // 2)
        def _():
            hear_front(2)

        @pl.when(i < tiles)
        def _():
            march(i)

        @pl.when(i >= lag)
        def _():
            finish(i - lag)

        return 0

    for copy in first_load:
        copy.wait()
    hear_front(0)
    lax.fori_loop(0, tiles + lag, step, 0)

    @pl.when(z < chips - 1)
    def _():
        pl.semaphore_wait(behind, (chips - 1 - z) * jnp.where(z == 0, 1 + sides, 1))

    @pl.when(z == 0)
    def _():
        def tell_level(chip, _):
            tell(level, 2 * chip + core, col)
            return 0

        lax.fori_loop(1, chips, tell_level, 0)

    def send_behind(i, _):
        chip_copy(i).start()
        return 0

    lax.fori_loop(z + 1, chips, send_behind, 0)

    @pl.when(z <= LEADERS)
    def _():
        pl.semaphore_wait(level, 1)

        def send_beside(i, _):
            send_border(i)
            return 0

        lax.fori_loop(z, chips, send_beside, 0)

    shape = (8, LANES)
    state = [[jnp.ones(shape, F32), jnp.ones(shape, F32)] + [jnp.zeros(shape, F32)] * 3 for _ in range(2)]
    for chip in range(chips):

        @pl.when(z != chip)
        def _():
            pltpu.make_async_remote_copy(
                src_ref=packed.at[0], dst_ref=got.at[chip], send_sem=chip_send, recv_sem=chip_recv.at[chip],
                device_id=device(slab, col), device_id_type=MESH,
            ).wait_recv()

        words = [got[chip, n] for n in range(5)]
        for half in range(2):
            codes = [(w & 0xFFFF) if half == 0 else (lax.shift_right_logical(w, 16)) for w in words]
            fine, plain, color, reach, coarse = state[half]
            color = color + fine * decode_log(codes[0], COLOR_SPAN)
            reach = reach + fine * decode_log(codes[1], DEPTH_SPAN)
            coarse = coarse + plain * decode_log(codes[3], COLOR_SPAN)
            fine = fine * (codes[2].astype(F32) * (1.0 / TOP))
            plain = plain * (codes[4].astype(F32) * (1.0 / TOP))
            state[half] = [fine, plain, color, reach, coarse]
    for half in range(2):
        fine, plain, color, reach, coarse = state[half]
        rows = pl.ds(8 * half, 8)
        image_out[0, rows] = color
        image_out[1, rows] = (reach - SHIFT * (1.0 - fine)) * (1.0 / 2048)
        image_out[2, rows] = coarse

    def all_borders(side, c):
        return pltpu.make_async_remote_copy(
            src_ref=border, dst_ref=border_got.at[side], send_sem=border_send.at[side], recv_sem=border_recv.at[side],
            device_id=device(slab, c), device_id_type=MESH,
        )

    both_sides(lambda side, c: all_borders(side, c).wait_recv())
    line = (1, LANES)
    fine, plain = jnp.ones(line, F32), jnp.ones(line, F32)
    color, reach, coarse = [jnp.zeros(line, F32)] * 3
    for chip in range(chips):
        parts = [
            jnp.where(left[:1], border_got[1, chip, pl.ds(n, 1)], border_got[0, chip, pl.ds(n, 1)]) for n in range(5)
        ]
        color, reach, coarse = color + fine * parts[0], reach + fine * parts[1], coarse + plain * parts[3]
        fine, plain = fine * parts[2], plain * parts[4]
    there = jnp.where(left, jnp.where(col < columns - 1, 1.0, 0.0), jnp.where(col > 0, 1.0, 0.0))
    for n, row in enumerate((color, (reach - SHIFT * (1.0 - fine)) * (1.0 / 2048), coarse)):
        row = jnp.where(there > 0.5, jnp.broadcast_to(row, (8, LANES)), 0.0)
        image_out[n, pl.ds(2 * 8, 8)] = pltpu.roll(row, LANES // 2, 1)

    @pl.when(slab > 0)
    def _():
        pltpu.make_async_remote_copy(
            src_ref=front, dst_ref=halo, send_sem=halo_send, recv_sem=halo_recv.at[0],
            device_id=device(slab - 1, col), device_id_type=MESH,
        ).wait_send()

    pltpu.make_async_remote_copy(
        src_ref=pool.at[:, 2], dst_ref=pool.at[:, core], send_sem=pair_send, recv_sem=pair_recv.at[0],
        device_id=device(other, col), device_id_type=MESH,
    ).wait_send()
    others = pl.ds(0, tiles - 1)
    pltpu.make_async_remote_copy(
        src_ref=packed.at[others], dst_ref=got.at[others], send_sem=chip_send, recv_sem=chip_recv.at[0],
        device_id=device(other, col), device_id_type=MESH,
    ).wait_send()
    both_sides(lambda side, c: all_borders(side, c).wait_send())


def smooth_kernel(image, color_out, depth_out, coarse_out, padded):
    half = LANES // 2
    for n, out in enumerate((color_out, depth_out, coarse_out)):
        whole = image[n]
        turned = pltpu.roll(whole, half, 1)
        padded[n, pl.ds(7, 1)] = whole[16:17]
        padded[n, pl.ds(8, HALF)] = whole[:HALF]
        padded[n, pl.ds(8 + HALF, HALF)] = turned[:HALF]
        padded[n, pl.ds(8 + 2 * HALF, 1)] = turned[16:17]
        smooth = 0.25 * padded[n, pl.ds(7, 32)] + 0.5 * padded[n, pl.ds(8, 32)] + 0.25 * padded[n, pl.ds(9, 32)]
        out[...] = smooth[:, :half]


def body(field, fine_plane, fine_frac, counts):
    channels, depth, rows, width = field.shape
    slots = fine_plane.shape[0]
    tiles = width // LANES
    dma = pltpu.SemaphoreType.DMA
    out = jax.ShapeDtypeStruct((rows, LANES // 2), F32)
    vmem = pl.BlockSpec(memory_space=pltpu.VMEM)
    anywhere = pl.BlockSpec(memory_space=pltpu.HBM)
    image = pl.pallas_call(
        kernel,
        out_shape=jax.ShapeDtypeStruct((3, 24, LANES), F32),
        in_specs=[anywhere] * 4,
        out_specs=vmem,
        scratch_shapes=[
            pltpu.VMEM((channels, depth, rows, width), jnp.bfloat16),
            pltpu.VMEM((channels, rows, width), jnp.bfloat16),
            pltpu.VMEM((channels, rows, width), jnp.bfloat16),
            pltpu.VMEM((slots, rows, width), jnp.int32),
            pltpu.VMEM((slots, rows, width), jnp.int32),
            pltpu.VMEM((1, rows, width), jnp.int32),
            pltpu.VMEM((tiles, 3, 5, HALF, LANES), F32),
            pltpu.VMEM((tiles, 5, 8, LANES), jnp.int32),
            pltpu.VMEM((tiles, 5, 8, LANES), jnp.int32),
            pltpu.VMEM((tiles, 8, LANES), F32),
            pltpu.VMEM((2, tiles, 8, LANES), F32),
            dma((5, 2)),
            dma, dma((3,)),
            dma, dma((tiles,)),
            dma, dma((tiles,)),
            dma((2,)), dma((2,)),
            pltpu.SemaphoreType.REGULAR, pltpu.SemaphoreType.REGULAR, pltpu.SemaphoreType.REGULAR,
        ],
        compiler_params=pltpu.CompilerParams(collective_id=0, has_side_effects=True, vmem_limit_bytes=56400000),
        name="render",
    )(field, fine_plane, fine_frac, counts)
    return pl.pallas_call(
        smooth_kernel,
        out_shape=(out, out, out),
        in_specs=[vmem],
        out_specs=(vmem, vmem, vmem),
        scratch_shapes=[pltpu.VMEM((3, rows + 16, LANES), F32)],
        compiler_params=pltpu.CompilerParams(vmem_limit_bytes=4 << 20),
        name="smooth",
    )(image)


def solution(mesh):
    in_specs = (
        P(None, "slab", "col", None),
        P("slab", "col", None),
        P("slab", "col", None),
        P("slab", "col", None),
    )
    out_specs = (P("col", "slab"), P("col", "slab"), P("col", "slab"))
    return jax.shard_map(body, mesh=mesh, in_specs=in_specs, out_specs=out_specs, check_vma=False)
```
